256 devices in a mesh: row: 64 (over x, z_lo, y), col: 4 (over z_hi, core).
Axes of the slice: x: 4, y: 4, z: 8 (z_hi: 2, z_lo: 4; z = z_hi * 4 + z_lo), core: 2. Of those that a mesh axis runs over, the one named last changes fastest.
Arguments:
- pair_rep: bfloat16 [1024, 1024, 128], P('row', 'col'), may hold values from -6 to 6
- chain_len: int32 [16], replicated, may hold values from 1 to 64, as said below
- tri_gain: float32 [128], replicated, may hold values from 0.5 to 2
- tri_in: bfloat16 [128, 640], replicated, may hold values from -0.5 to 0.5
- sum_gain: float32 [128], replicated, may hold values from 0.5 to 2
- tri_out: bfloat16 [128, 128], replicated, may hold values from -0.5 to 0.5
- att_gain: float32 [128], replicated, may hold values from 0.5 to 8
- att_in: bfloat16 [128, 512], replicated, may hold values from -0.5 to 0.5
- att_bias: bfloat16 [128, 4], replicated, may hold values from -2 to 2
- att_out: bfloat16 [128, 128], replicated, may hold values from -4 to 4
Outputs:
- new_pair: bfloat16 [1024, 1024, 128], P('row', 'col')
The draws below stay inside these ranges and needn't reach their ends.
Inputs may be any that keep to these rules, and one draw needn't show every extreme that they name: `chain_len`: one chain in every draw has all 64 slots live.
All inputs are finite; a program needn't handle non-finite values.
Results may differ from the reference program's by a relative error of at most 0.039.
The reference program's roundings to bfloat16 on the way count: a program that leaves them out, or rounds other values in their place, can miss the bound.
Values may be sent and summed in bfloat16 or wider, within the bound.
A program may use at most 128 MiB of HBM per device.

```python
import math
import jax
import jax.numpy as jnp
from jax import lax

C = 128
CH = 128
H = 4
DH = 32
TOK_ROW = 16
KCD = 16
SLOT = 64
N_TOK = 1024
COLBLK = 256
KC = 64
NCHAIN = 16
HD = 128
N_COL = 4


def draw_chain_len(key, part):
    key_lengths = jax.random.fold_in(key, 11)
    key_full = jax.random.fold_in(key, 12)
    lengths = jax.random.randint(key_lengths, (NCHAIN,), 1, SLOT + 1, dtype=jnp.int32)
    full_chain = jax.random.randint(key_full, (), 0, NCHAIN, dtype=jnp.int32)
    return lengths.at[full_chain].set(SLOT)


def draw_att_gain(key, part):
    return jax.random.uniform(key, (C,), jnp.float32, 0.5, 2.0)


def block_scale(key, shape, split, smallest, top_value):
    gain = 1.0
    for axis_at, blocks in split:
        draws = jax.random.uniform(jax.random.fold_in(jax.random.fold_in(key, 6), axis_at), (blocks,), jnp.float32, smallest / len(split), top_value / len(split))
        gain = gain * jnp.repeat(jnp.exp(draws), shape[axis_at] // blocks).reshape((-1,) + (1,) * (len(shape) - 1 - axis_at))
    return gain


def normal_values(rng, shape, deviation, bound, shards=(), held_as=jnp.bfloat16):
    factor_of = block_scale(rng, shape, shards, -0.22, 0.18) if shards else 1.0
    entries = jax.random.normal(rng, shape, jnp.float32) * deviation * factor_of
    return jnp.minimum(jnp.maximum(entries, -bound), bound).astype(held_as)


def setup_inputs(seed: int = 0) -> dict:
    streams_of = jax.random.split(jax.random.key(seed), 11)
    pair_rep = normal_values(streams_of[0], (N_TOK, N_TOK, C), 1.0, 6.0, ((0, 64), (1, 4)))
    chain_len = draw_chain_len(jax.random.fold_in(streams_of[10], 71), 0)
    tri_gain = jnp.clip(jax.random.uniform(streams_of[2], (C,), jnp.float32, 0.5, 2.0), 0.5, 2.0)
    tri_in = normal_values(streams_of[3], (C, 4 * CH + C), C ** -0.5, 0.5)
    sum_gain = jnp.clip(jax.random.uniform(streams_of[4], (CH,), jnp.float32, 0.5, 2.0), 0.5, 2.0)
    tri_out = normal_values(streams_of[5], (CH, C), CH ** -0.5, 0.5)
    att_gain = draw_att_gain(jax.random.fold_in(streams_of[10], 71), 0)
    att_in = normal_values(streams_of[7], (C, 4 * HD), C ** -0.5, 0.5)
    att_bias = normal_values(streams_of[8], (C, H), (max(1, C // 16)) ** -0.5, 2.0)
    att_out = normal_values(streams_of[9], (HD, C), (max(1, H * DH // 64)) ** -0.5, 4.0)
    return {"pair_rep": pair_rep, "chain_len": chain_len, "tri_gain": tri_gain, "tri_in": tri_in, "sum_gain": sum_gain, "tri_out": tri_out, "att_gain": att_gain, "att_in": att_in, "att_bias": att_bias, "att_out": att_out}


EPSILON = 1e-05
NEG_SCORE = -1e+30

def layer_norm(values, norm_gain):
    values = values.astype(jnp.float32)
    centre = values - lax.optimization_barrier(jnp.mean(values, axis=-1, keepdims=True))
    spread = lax.optimization_barrier(jnp.mean(centre * centre, axis=-1, keepdims=True))
    return centre * lax.rsqrt(spread + EPSILON) * norm_gain

def reference(pair_rep, chain_len, tri_gain, tri_in, sum_gain, tri_out, att_gain, att_in, att_bias, att_out):
    positions = lax.broadcasted_iota(jnp.int32, (NCHAIN, SLOT), 1)
    live_mask = (positions < chain_len[:, None]).astype(jnp.float32).reshape(N_TOK)
    group_pair = pair_rep.reshape(N_TOK, N_COL, COLBLK, C)[:, :, :KCD].reshape(N_TOK, KC, C)
    group_live = live_mask.reshape(N_COL, COLBLK)[:, :KCD].reshape(KC)
    group_norm = layer_norm(group_pair, tri_gain).astype(jnp.bfloat16)
    group_proj = jnp.dot(group_norm, tri_in[:, :4 * CH], preferred_element_type=jnp.float32)
    pair_live = live_mask[:, None, None] * group_live[None, :, None]
    left_edge = (jax.nn.sigmoid(group_proj[..., :CH]) * group_proj[..., CH:2 * CH] * pair_live).astype(jnp.bfloat16)
    right_edge = (jax.nn.sigmoid(group_proj[..., 2 * CH:3 * CH]) * group_proj[..., 3 * CH:4 * CH] * pair_live).astype(jnp.bfloat16)
    right_wide = right_edge.astype(jnp.float32)
    starts = jnp.arange(N_TOK // TOK_ROW, dtype=jnp.int32) * TOK_ROW

    def triangle_block(row_first):
        rows_pair = lax.dynamic_slice_in_dim(pair_rep, row_first, TOK_ROW, 0)
        rows_left = lax.dynamic_slice_in_dim(left_edge, row_first, TOK_ROW, 0)
        rows_norm = layer_norm(rows_pair, tri_gain).astype(jnp.bfloat16)
        out_gate = jax.nn.sigmoid(jnp.dot(rows_norm, tri_in[:, 4 * CH:], preferred_element_type=jnp.float32))
        tri_sum = jnp.einsum('ikc,jkc->ijc', rows_left.astype(jnp.float32), right_wide, precision=lax.Precision.HIGHEST)
        sum_norm = layer_norm(tri_sum, sum_gain).astype(jnp.bfloat16)
        update = jnp.dot(sum_norm, tri_out, preferred_element_type=jnp.float32)
        return (rows_pair.astype(jnp.float32) + out_gate * update).astype(jnp.bfloat16)
    mid_pair = lax.map(triangle_block, starts).reshape(N_TOK, N_TOK, C)

    def bias_block(row_first):
        rows_pair = lax.dynamic_slice_in_dim(mid_pair, row_first, TOK_ROW, 0)
        rows_norm = layer_norm(rows_pair, att_gain).astype(jnp.bfloat16)
        return jnp.dot(rows_norm, att_bias, preferred_element_type=jnp.float32).astype(jnp.bfloat16)
    pair_bias = jnp.transpose(lax.map(bias_block, starts).reshape(N_TOK, N_TOK, H), (2, 0, 1))
    key_mask = live_mask > 0.5

    def attend_row(row_pair):
        row_norm = layer_norm(row_pair, att_gain).astype(jnp.bfloat16)
        projected = jnp.dot(row_norm, att_in, preferred_element_type=jnp.float32)
        queries = projected[:, :HD].astype(jnp.bfloat16).reshape(N_TOK, H, DH)
        keys = projected[:, HD:2 * HD].astype(jnp.bfloat16).reshape(N_TOK, H, DH)
        values = projected[:, 2 * HD:3 * HD].astype(jnp.bfloat16).reshape(N_TOK, H, DH)
        att_gate = jax.nn.sigmoid(projected[:, 3 * HD:])
        scores = jnp.einsum('jhd,khd->hjk', queries.astype(jnp.float32), keys.astype(jnp.float32), precision=lax.Precision.HIGHEST) / math.sqrt(DH) + pair_bias
        scores = jnp.where(key_mask[None, None, :], scores, NEG_SCORE)
        row_top = lax.optimization_barrier(jnp.max(scores, axis=-1, keepdims=True))
        weights = jnp.exp(scores - row_top).astype(jnp.bfloat16)
        totals = lax.optimization_barrier(jnp.sum(weights.astype(jnp.float32), axis=-1))
        summed = jnp.einsum('hjk,khd->jhd', weights.astype(jnp.float32), values.astype(jnp.float32), precision=lax.Precision.HIGHEST)
        attended = summed / jnp.transpose(totals)[:, :, None]
        attended = (attended.reshape(N_TOK, HD) * att_gate).astype(jnp.bfloat16)
        return (row_pair.astype(jnp.float32) + jnp.dot(attended, att_out, preferred_element_type=jnp.float32)).astype(jnp.bfloat16)
    return lax.map(attend_row, mid_pair)
```

```python
import math

import jax
import jax.numpy as jnp
from jax import lax
from jax.experimental import pallas as pl
from jax.experimental.pallas import tpu as pltpu
from jax.sharding import PartitionSpec as P

CH = 128
H = 4
DH = 32
KCD = 16
SLOT = 64
EPSILON = 1e-05
NEG_SCORE = -1e30
MESH = pl.DeviceIdType.MESH
F32 = jnp.float32
BF16 = jnp.bfloat16


def layer_norm(values, norm_gain):
    values = values.astype(F32)
    centre = values - jnp.mean(values, axis=-1, keepdims=True)
    spread = jnp.mean(centre * centre, axis=-1, keepdims=True)
    return centre * lax.rsqrt(spread + EPSILON) * norm_gain


def live_tokens(chain_len):
    positions = lax.broadcasted_iota(jnp.int32, (chain_len.shape[0], SLOT), 1)
    return (positions < chain_len[:, None]).astype(F32).reshape(-1)


def place():
    row = lax.axis_index("row")
    col = lax.axis_index("col")
    return row // 16, (row // 4) % 4, row % 4, col


def device(x, zl, y, col):
    return (x * 16 + zl * 4 + y, col)


class Spread:
    def __init__(self, pay, buf, s1_send, s1_recv, ring_send, ring_recv):
        self.pay, self.buf = pay, buf
        self.s1_send, self.s1_recv = s1_send, s1_recv
        self.ring_send, self.ring_recv = ring_send, ring_recv
        self.x, self.zl, self.y, self.col = place()
        self.sent = []

    def partner(self, i):
        return device(self.col, (self.zl + i) % 4, self.y, self.x)

    def neighbour(self, h, axis, d):
        along_y = (h == 0) == (axis == 0)
        if along_y:
            return device(self.x, self.zl, (self.y + d + 4) % 4, self.col)
        return device((self.x + d + 4) % 4, self.zl, self.y, self.col)

    def greet(self, barrier):
        def hello(to):
            pl.semaphore_signal(barrier, inc=1, device_id=to, device_id_type=MESH)

        for i in range(1, 4):
            hello(self.partner(i))
        for axis in range(2):
            for d in (1, -1):
                hello(self.neighbour(0, axis, d))

        @pl.when(self.x != self.col)
        def _():
            hello(self.partner(0))

        return 7 + (self.x != self.col).astype(jnp.int32)

    def first(self, i):
        return pltpu.make_async_remote_copy(
            src_ref=self.pay,
            dst_ref=self.buf.at[:, self.col, self.y, self.zl],
            send_sem=self.s1_send.at[i],
            recv_sem=self.s1_recv.at[i],
            device_id=self.partner(i),
            device_id_type=MESH,
        )

    def first_local(self):
        return pltpu.make_async_copy(
            self.pay, self.buf.at[:, self.col, self.y, self.zl], self.s1_send.at[0]
        )

    def first_arrival(self, i):
        return pltpu.make_async_remote_copy(
            src_ref=self.pay,
            dst_ref=self.buf.at[:, self.x, self.y, (self.zl + 4 - i) % 4],
            send_sem=self.s1_send.at[i],
            recv_sem=self.s1_recv.at[i],
            device_id=self.partner(i),
            device_id_type=MESH,
        )

    def start(self):
        @pl.when(self.x != self.col)
        def _():
            self.first(0).start()

        @pl.when(self.x == self.col)
        def _():
            self.first_local().start()

        for i in range(1, 4):
            self.first(i).start()

    def landed(self):
        @pl.when(self.x != self.col)
        def _():
            self.first_arrival(0).wait_recv()
            self.first(0).wait_send()

        @pl.when(self.x == self.col)
        def _():
            self.first_local().wait()

        for i in range(1, 4):
            self.first_arrival(i).wait_recv()

    def piece(self, h, f, s, sub):
        xi, yi = (s, f) if h == 0 else (f, s)
        return self.buf.at[h, (self.x + xi) % 4, (self.y + yi) % 4, pl.ds(2 * sub, 2)]

    def slot(self, h, f, s, sub):
        return ((h * 4 + f) * 4 + s) * 2 + sub

    def send(self, h, f, s, sub, axis, d):
        there = ((f - d) % 4, s) if axis == 0 else (f, (s - d) % 4)
        copy = pltpu.make_async_remote_copy(
            src_ref=self.piece(h, f, s, sub),
            dst_ref=self.piece(h, f, s, sub),
            send_sem=self.ring_send.at[len(self.sent)],
            recv_sem=self.ring_recv.at[self.slot(h, *there, sub)],
            device_id=self.neighbour(h, axis, d),
            device_id_type=MESH,
        )
        copy.start()
        self.sent.append(copy)

    def own(self):
        for axis in range(2):
            for step in range(2):
                for h in range(2):
                    self.send(h, 0, 0, step, axis, 1)
                    self.send(h, 0, 0, 1 - step, axis, -1)

    def arrive(self, h, f, s, sub):
        pltpu.make_async_remote_copy(
            src_ref=self.piece(h, f, s, sub),
            dst_ref=self.piece(h, f, s, sub),
            send_sem=self.ring_send.at[0],
            recv_sem=self.ring_recv.at[self.slot(h, f, s, sub)],
            device_id=self.neighbour(h, 0, 1),
            device_id_type=MESH,
        ).wait_recv()

    def take(self, h, f, s, sub):
        self.arrive(h, f, s, sub)
        if s == 0:
            if f == 3 and sub == 0:
                self.send(h, f, s, sub, 0, 1)
            if f == 1 and sub == 1:
                self.send(h, f, s, sub, 0, -1)
            self.send(h, f, s, sub, 1, 1 if sub == 0 else -1)
            self.send(h, f, s, sub, 1, -1 if sub == 0 else 1)
        else:
            if s == 3 and sub == 0:
                self.send(h, f, s, sub, 1, 1)
            if s == 1 and sub == 1:
                self.send(h, f, s, sub, 1, -1)

    def order(self):
        near = [(3, 0), (1, 1), (3, 1), (1, 0)]
        steps = [(a, 0, sub) for a, sub in near]
        steps += [(0, a, sub) for a, sub in near]
        steps += [(2, 0, 0), (2, 0, 1)]
        for f in (3, 1):
            steps += [(f, a, sub) for a, sub in near]
        steps += [(0, 2, 0), (0, 2, 1)]
        steps += [(2, a, sub) for a, sub in near]
        steps += [(f, 2, sub) for f in (3, 1, 2) for sub in range(2)]
        return [(h, *step) for step in steps for h in range(2)]

    def finish(self):
        for i in range(1, 4):
            self.first(i).wait_send()
        for copy in self.sent:
            copy.wait_send()


SPREAD_SEMS = [
    pltpu.SemaphoreType.DMA((4,)),
    pltpu.SemaphoreType.DMA((4,)),
    pltpu.SemaphoreType.DMA((60,)),
    pltpu.SemaphoreType.DMA((64,)),
]


def edge_exchange(right, left, right_all, left_all, s1s, s1r, rs, rr, l_send, l_recv, l_own):
    spread = Spread(right, right_all, s1s, s1r, rs, rr)
    x, zl, y, col = spread.x, spread.zl, spread.y, spread.col
    barrier = pltpu.get_barrier_semaphore()
    count = spread.greet(barrier)
    peers = [device(x, zl, y, col ^ 1), device(x, zl, y, col ^ 2), device(x, zl, y, col ^ 3)]
    for peer in peers:
        pl.semaphore_signal(barrier, inc=1, device_id=peer, device_id_type=MESH)
    pl.semaphore_wait(barrier, count + 3)
    spread.start()

    def left_copy(j, block):
        return pltpu.make_async_remote_copy(
            src_ref=left,
            dst_ref=left_all.at[block],
            send_sem=l_send.at[j],
            recv_sem=l_recv.at[j],
            device_id=peers[j],
            device_id_type=MESH,
        )

    for j in range(3):
        left_copy(j, col).start()
    own = pltpu.make_async_copy(left, left_all.at[col], l_own.at[0])
    own.start()
    spread.landed()
    spread.own()
    for step in spread.order():
        spread.take(*step)
    own.wait()
    for j in range(3):
        left_copy(j, col).wait_send()
        left_copy(j, col ^ (j + 1)).wait_recv()
    spread.finish()


def norm_exchange(bias, norm, bias_all, norm_all, held, s1s, s1r, rs, rr, sib, hop1s, hop1r, hop2s, hop2r, fwds, fwdr):
    spread = Spread(bias, bias_all, s1s, s1r, rs, rr)
    x, zl, y, col = spread.x, spread.zl, spread.y, spread.col
    core = col % 2
    z = (col // 2) * 4 + zl

    def at_z(offset):
        there = (z + offset + 8) % 8
        return device(x, there % 4, y, (there // 4) * 2 + core)

    def col_at(offset):
        return (((z + offset + 8) % 8) // 4) * 2 + core

    sibling = device(x, zl, y, col ^ 1)
    barrier = pltpu.get_barrier_semaphore()
    count = spread.greet(barrier)
    for peer in (sibling, at_z(2), at_z(-2)):
        pl.semaphore_signal(barrier, inc=1, device_id=peer, device_id_type=MESH)
    pl.semaphore_wait(barrier, count + 3)

    def remote(src, dst, send, recv, to):
        return pltpu.make_async_remote_copy(
            src_ref=src, dst_ref=dst, send_sem=send, recv_sem=recv, device_id=to, device_id_type=MESH
        )

    def rows(way, c):
        return pl.ds(8 * way + 2 * c, 2)

    def step(way):
        return 2 if way == 0 else -2

    def hop1(way, c):
        return remote(
            norm.at[rows(way, c)], held.at[way, c], hop1s.at[way, c], hop1r.at[way, c], at_z(step(way))
        )

    def hop2(way, c):
        return remote(
            held.at[way, c],
            norm_all.at[col_at(-step(way)), rows(way, c)],
            hop2s.at[way, c],
            hop2r.at[way, c],
            at_z(step(way)),
        )

    def hop2_arrival(way, c):
        return remote(
            held.at[way, c],
            norm_all.at[col ^ 2, rows(way, c)],
            hop2s.at[way, c],
            hop2r.at[way, c],
            at_z(step(way)),
        )

    def forward(way, c, block):
        return remote(
            norm_all.at[col ^ 2, rows(way, c)],
            norm_all.at[block, rows(way, c)],
            fwds.at[way, c],
            fwdr.at[way, c],
            sibling,
        )

    spread.start()
    for c in range(4):
        for way in range(2):
            hop1(way, c).start()
    own = pltpu.make_async_copy(norm, norm_all.at[col], sib.at[0])
    own.start()
    to_sibling = remote(norm, norm_all.at[col], sib.at[1], sib.at[2], sibling)
    to_sibling.start()
    spread.landed()
    spread.own()

    def relay(way, c):
        hop1(way, c).wait_recv()
        hop2(way, c).start()

    def last(way, c):
        hop2_arrival(way, c).wait_recv()
        forward(way, c, col ^ 2).start()

    extra = []
    for c in range(5):
        for way in range(2):
            if c < 4:
                extra.append((relay, way, c))
        for way in range(2):
            if c > 0:
                extra.append((last, way, c - 1))
    order = spread.order()
    for at, each in enumerate(order):
        spread.take(*each)
        if at % 4 == 3 and extra:
            fn, way, c = extra.pop(0)
            fn(way, c)
    for fn, way, c in extra:
        fn(way, c)
    own.wait()
    to_sibling.wait_send()
    remote(norm, norm_all.at[col ^ 1], sib.at[1], sib.at[2], sibling).wait_recv()
    for c in range(4):
        for way in range(2):
            hop1(way, c).wait_send()
            hop2(way, c).wait_send()
            forward(way, c, col ^ 2).wait_send()
            forward(way, c, col ^ 3).wait_recv()
    spread.finish()


ANY = pl.BlockSpec(memory_space=pl.ANY)


def exchange_edges(right, left):
    return pl.pallas_call(
        edge_exchange,
        name="edge_exchange",
        out_shape=(
            jax.ShapeDtypeStruct((2, 4, 4, 4) + right.shape[1:], right.dtype),
            jax.ShapeDtypeStruct((4,) + left.shape, left.dtype),
        ),
        in_specs=[ANY, ANY],
        out_specs=(ANY, ANY),
        scratch_shapes=SPREAD_SEMS
        + [
            pltpu.SemaphoreType.DMA((3,)),
            pltpu.SemaphoreType.DMA((3,)),
            pltpu.SemaphoreType.DMA((1,)),
        ],
        compiler_params=pltpu.CompilerParams(collective_id=0, has_side_effects=True),
    )(right, left)


def exchange_norms(bias, norm):
    return pl.pallas_call(
        norm_exchange,
        name="norm_exchange",
        out_shape=(
            jax.ShapeDtypeStruct((2, 4, 4, 4) + bias.shape[1:], bias.dtype),
            jax.ShapeDtypeStruct((4,) + norm.shape, norm.dtype),
        ),
        in_specs=[ANY, ANY],
        out_specs=(ANY, ANY),
        scratch_shapes=[pltpu.VMEM((2, 4, 2) + norm.shape[1:], norm.dtype)]
        + SPREAD_SEMS
        + [pltpu.SemaphoreType.DMA((3,))]
        + [pltpu.SemaphoreType.DMA((2, 4))] * 6,
        compiler_params=pltpu.CompilerParams(collective_id=1, has_side_effects=True),
    )(bias, norm)


def triangle_kernel(
    right, left, pair, tri_gain, tri_in, sum_gain, tri_out, att_gain, att_bias,
    mid, norm, bias, left_wide, normed, bias_wide,
):
    at = pl.program_id(0)

    @pl.when(at == 0)
    def _():
        for b in range(4):
            left_wide[pl.ds(16 * b, 16)] = left[b].astype(F32)

    def contract(q, sums):
        block, half = q // 2, q % 2
        sums = list(sums)
        for k in range(8):
            edge = right[half, block, 0, 0, k].astype(F32)
            token = block * 16 + half * 8 + k
            for i in range(16):
                sums[i] = sums[i] + edge * left_wide[token, pl.ds(i, 1), :]
        return tuple(sums)

    zero = jnp.zeros((16, CH), F32)
    sums = lax.fori_loop(0, 8, contract, (zero,) * 16)
    for i in range(16):
        normed[i] = layer_norm(sums[i], sum_gain[...]).astype(BF16)
    update = jnp.dot(normed[...].reshape(256, CH), tri_out[...], preferred_element_type=F32)
    tile = pair[...].reshape(256, CH).astype(F32)
    tri_norm = layer_norm(tile, tri_gain[...]).astype(BF16)
    gate = jax.nn.sigmoid(jnp.dot(tri_norm, tri_in[...], preferred_element_type=F32))
    mid_tile = (tile + gate * update).astype(BF16)
    mid[...] = mid_tile.reshape(16, 16, CH)
    att = layer_norm(mid_tile, att_gain[...]).astype(BF16)
    norm[:, pl.ds(pl.multiple_of(at * 16, 16), 16), :] = att.reshape(16, 16, CH)

    @pl.when(at == 15)
    def _():
        for i in range(16):
            rows = lax.dot_general(
                att_bias[...], norm[i], (((1,), (1,)), ((), ())), preferred_element_type=F32
            )
            for h in range(H):
                bias_wide[h, pl.ds(i, 1), :] = rows[h : h + 1]
        for h in range(H):
            bias[h // 2, h % 2] = bias_wide[h].astype(BF16)


def triangle(right_all, left_all, pair_rep, tri_gain, tri_in, sum_gain, tri_out, att_gain, att_bias):
    whole = lambda *shape: pl.BlockSpec(shape, lambda t: (0,) * len(shape))
    bias_rows = jnp.zeros((8, CH), BF16).at[:H].set(att_bias.T)
    return pl.pallas_call(
        triangle_kernel,
        name="triangle",
        grid=(16,),
        out_shape=(
            jax.ShapeDtypeStruct((16, 256, CH), BF16),
            jax.ShapeDtypeStruct((16, 256, CH), BF16),
            jax.ShapeDtypeStruct((2, 2, 16, 256), BF16),
        ),
        in_specs=[
            pl.BlockSpec((2, 4, 1, 1, 8, 16, CH), lambda t: (0, 0, t % 4, t // 4, 0, 0, 0)),
            whole(4, 16, 16, CH),
            pl.BlockSpec((16, 16, CH), lambda t: (0, t, 0)),
            whole(1, CH),
            pl.BlockSpec((CH, CH), lambda t: (0, 4)),
            whole(1, CH),
            whole(CH, CH),
            whole(1, CH),
            whole(8, CH),
        ],
        out_specs=(
            pl.BlockSpec((16, 16, CH), lambda t: (0, t, 0)),
            whole(16, 256, CH),
            whole(2, 2, 16, 256),
        ),
        scratch_shapes=[
            pltpu.VMEM((64, 16, CH), F32),
            pltpu.VMEM((16, 16, CH), BF16),
            pltpu.VMEM((H, 16, 256), F32),
        ],
        compiler_params=pltpu.CompilerParams(vmem_limit_bytes=32 << 20),
    )(
        right_all, left_all, pair_rep, tri_gain.reshape(1, CH), tri_in, sum_gain.reshape(1, CH),
        tri_out, att_gain.reshape(1, CH), bias_rows,
    )


TILE = 128


def attention_kernel(own, norm, mid, bias, dead, att_in, att_out, new, bias_wide):
    row = pl.program_id(0)

    @pl.when(row == 0)
    def _():
        for h in range(H):
            for block in range(4):
                masked = dead[:, pl.ds(256 * block, 256)]
                for part in range(16):
                    some = bias[h // 2, block, part % 4, part // 4, h % 2].astype(F32)
                    bias_wide[h, pl.ds(16 * part, 16), pl.ds(256 * block, 256)] = some + masked

    here = norm[...].reshape(4 * 256, CH)
    kv = jnp.dot(here, att_in[:, CH : 3 * CH], preferred_element_type=F32).astype(BF16)
    keys = kv[:, :CH]
    values = jnp.concatenate([kv[:, CH:], jnp.ones((1024, CH), BF16)], axis=1)
    mine = own[0]
    queries = jnp.dot(mine, att_in[:, :CH], preferred_element_type=F32).astype(BF16)
    gate = jax.nn.sigmoid(jnp.dot(mine, att_in[:, 3 * CH :], preferred_element_type=F32))
    lane_head = lax.broadcasted_iota(jnp.int32, (TILE, CH), 1) // DH
    for t in range(256 // TILE):
        rows = slice(t * TILE, (t + 1) * TILE)
        attended = jnp.zeros((TILE, CH), F32)
        for h in range(H):
            query = jnp.where(lane_head == h, queries[rows], jnp.zeros((), BF16))
            scores = lax.dot_general(
                query, keys, (((1,), (1,)), ((), ())), preferred_element_type=F32
            )
            scores = scores * (1.0 / math.sqrt(DH)) + bias_wide[h, pl.ds(t * TILE, TILE), :]
            top = jnp.max(scores, axis=-1, keepdims=True)
            weights = jnp.exp(scores - top).astype(BF16)
            summed = jnp.dot(weights, values, preferred_element_type=F32)
            attended = jnp.where(lane_head == h, summed[:, :CH] / summed[:, CH:], attended)
        attended = (attended * gate[rows]).astype(BF16)
        add = jnp.dot(attended, att_out[...], preferred_element_type=F32)
        new[0, pl.ds(t * TILE, TILE), :] = (mid[0, pl.ds(t * TILE, TILE), :].astype(F32) + add).astype(BF16)


def attention(own, norm_all, mid, bias_all, dead, att_in, att_out):
    whole = lambda *shape: pl.BlockSpec(shape, lambda t: (0,) * len(shape))
    one_row = pl.BlockSpec((1, 256, CH), lambda t: (t, 0, 0))
    return pl.pallas_call(
        attention_kernel,
        name="attention",
        grid=(16,),
        out_shape=jax.ShapeDtypeStruct((16, 256, CH), BF16),
        in_specs=[
            one_row,
            pl.BlockSpec((4, 1, 256, CH), lambda t: (0, t, 0, 0)),
            one_row,
            whole(2, 4, 4, 4, 2, 16, 256),
            whole(1, 1024),
            whole(CH, 4 * CH),
            whole(CH, CH),
        ],
        out_specs=one_row,
        scratch_shapes=[pltpu.VMEM((H, 256, 1024), F32)],
        compiler_params=pltpu.CompilerParams(vmem_limit_bytes=48 << 20),
    )(own, norm_all, mid, bias_all, dead, att_in, att_out)


def body(
    pair_rep, chain_len, tri_gain, tri_in, sum_gain, tri_out, att_gain, att_in, att_bias, att_out
):
    row_count = pair_rep.shape[0]
    col_count = pair_rep.shape[1]
    live_all = live_tokens(chain_len)
    live_rows = lax.dynamic_slice_in_dim(live_all, lax.axis_index("row") * row_count, row_count)
    live_cols = lax.dynamic_slice_in_dim(live_all, lax.axis_index("col") * col_count, KCD)
    group_norm = layer_norm(pair_rep[:, :KCD], tri_gain).astype(BF16)
    group_proj = jnp.dot(group_norm, tri_in[:, : 4 * CH], preferred_element_type=F32)
    pair_live = live_rows[:, None, None] * live_cols[None, :, None]
    left_edge = (jax.nn.sigmoid(group_proj[..., :CH]) * group_proj[..., CH : 2 * CH] * pair_live).astype(BF16)
    right_edge = (
        jax.nn.sigmoid(group_proj[..., 2 * CH : 3 * CH]) * group_proj[..., 3 * CH :] * pair_live
    ).astype(BF16)
    left_edge = jnp.transpose(left_edge, (1, 0, 2))
    right_edge = jnp.transpose(right_edge, (1, 0, 2)).reshape(2, 8, 16, CH)
    right_all, left_all = exchange_edges(right_edge, left_edge)
    mid, norm, bias = triangle(
        right_all, left_all, pair_rep, tri_gain, tri_in, sum_gain, tri_out, att_gain, att_bias
    )
    bias_all, norm_all = exchange_norms(bias, norm)
    dead = jnp.where(live_all > 0.5, 0.0, NEG_SCORE).reshape(1, -1)
    return attention(norm, norm_all, mid, bias_all, dead, att_in, att_out)


def solution(mesh):
    placed = (P("row", "col", None), P(), P(), P(), P(), P(), P(), P(), P(), P())
    return jax.shard_map(
        body, mesh=mesh, in_specs=placed, out_specs=P("row", "col", None), check_vma=False
    )
```

```python
import math

import jax
import jax.numpy as jnp
from jax import lax
from jax.experimental import pallas as pl
from jax.experimental.pallas import tpu as pltpu
from jax.sharding import PartitionSpec as P

CH = 128
H = 4
DH = 32
KCD = 16
SLOT = 64
EPSILON = 1e-05
NEG_SCORE = -1e30
MESH = pl.DeviceIdType.MESH
F32 = jnp.float32
BF16 = jnp.bfloat16


def layer_norm(values, norm_gain):
    values = values.astype(F32)
    centre = values - jnp.mean(values, axis=-1, keepdims=True)
    spread = jnp.mean(centre * centre, axis=-1, keepdims=True)
    return centre * lax.rsqrt(spread + EPSILON) * norm_gain


def live_tokens(chain_len):
    positions = lax.broadcasted_iota(jnp.int32, (chain_len.shape[0], SLOT), 1)
    return (positions < chain_len[:, None]).astype(F32).reshape(-1)


def place():
    row = lax.axis_index("row")
    col = lax.axis_index("col")
    return row // 16, (row // 4) % 4, row % 4, col


def device(x, zl, y, col):
    return (x * 16 + zl * 4 + y, col)


class Spread:
    def __init__(self, pay, buf, s1_send, s1_recv, ring_send, ring_recv):
        self.pay, self.buf = pay, buf
        self.s1_send, self.s1_recv = s1_send, s1_recv
        self.ring_send, self.ring_recv = ring_send, ring_recv
        self.x, self.zl, self.y, self.col = place()
        self.swapped = self.x != self.col
        self.sent = []

    def partner(self):
        return device(self.col, self.zl, self.y, self.x)

    def line(self, i):
        return device(self.x, (self.zl + i) % 4, self.y, self.col)

    def neighbour(self, h, axis, d):
        along_y = (h == 0) == (axis == 0)
        if along_y:
            return device(self.x, self.zl, (self.y + d + 4) % 4, self.col)
        return device((self.x + d + 4) % 4, self.zl, self.y, self.col)

    def greet(self, barrier):
        def hello(to):
            pl.semaphore_signal(barrier, inc=1, device_id=to, device_id_type=MESH)

        for i in range(1, 4):
            hello(self.line(i))
        for axis in range(2):
            for d in (1, -1):
                hello(self.neighbour(0, axis, d))

        @pl.when(self.swapped)
        def _():
            hello(self.partner())

        return 7 + self.swapped.astype(jnp.int32)

    def swap(self, arrival):
        into = (self.x, self.zl) if arrival else (self.col, self.zl)
        return pltpu.make_async_remote_copy(
            src_ref=self.pay,
            dst_ref=self.buf.at[:, into[0], self.y, into[1]],
            send_sem=self.s1_send.at[0],
            recv_sem=self.s1_recv.at[0],
            device_id=self.partner(),
            device_id_type=MESH,
        )

    def keep(self):
        return pltpu.make_async_copy(
            self.pay, self.buf.at[:, self.x, self.y, self.zl], self.s1_send.at[0]
        )

    def share(self, i, arrival):
        block = self.buf.at[:, self.x, self.y, (self.zl + 4 - i) % 4 if arrival else self.zl]
        return pltpu.make_async_remote_copy(
            src_ref=block,
            dst_ref=block,
            send_sem=self.s1_send.at[i],
            recv_sem=self.s1_recv.at[i],
            device_id=self.line(i),
            device_id_type=MESH,
        )

    def start(self):
        @pl.when(self.swapped)
        def _():
            self.swap(False).start()

        @pl.when(jnp.logical_not(self.swapped))
        def _():
            self.keep().start()

    def landed(self):
        @pl.when(self.swapped)
        def _():
            self.swap(True).wait_recv()
            self.swap(False).wait_send()

        @pl.when(jnp.logical_not(self.swapped))
        def _():
            self.keep().wait()

        for i in (1, 3, 2):
            self.share(i, False).start()
        for i in (1, 3, 2):
            self.share(i, True).wait_recv()

    def piece(self, h, f, s, sub):
        xi, yi = (s, f) if h == 0 else (f, s)
        return self.buf.at[h, (self.x + xi) % 4, (self.y + yi) % 4, pl.ds(2 * sub, 2)]

    def slot(self, h, f, s, sub):
        return ((h * 4 + f) * 4 + s) * 2 + sub

    def send(self, h, f, s, sub, axis, d):
        there = ((f - d) % 4, s) if axis == 0 else (f, (s - d) % 4)
        copy = pltpu.make_async_remote_copy(
            src_ref=self.piece(h, f, s, sub),
            dst_ref=self.piece(h, f, s, sub),
            send_sem=self.ring_send.at[len(self.sent)],
            recv_sem=self.ring_recv.at[self.slot(h, *there, sub)],
            device_id=self.neighbour(h, axis, d),
            device_id_type=MESH,
        )
        copy.start()
        self.sent.append(copy)

    def own(self):
        for axis in range(2):
            for step in range(2):
                for h in range(2):
                    self.send(h, 0, 0, step, axis, 1)
                    self.send(h, 0, 0, 1 - step, axis, -1)

    def arrive(self, h, f, s, sub):
        pltpu.make_async_remote_copy(
            src_ref=self.piece(h, f, s, sub),
            dst_ref=self.piece(h, f, s, sub),
            send_sem=self.ring_send.at[0],
            recv_sem=self.ring_recv.at[self.slot(h, f, s, sub)],
            device_id=self.neighbour(h, 0, 1),
            device_id_type=MESH,
        ).wait_recv()

    def take(self, h, f, s, sub):
        self.arrive(h, f, s, sub)
        if s == 0:
            if f == 3 and sub == 0:
                self.send(h, f, s, sub, 0, 1)
            if f == 1 and sub == 1:
                self.send(h, f, s, sub, 0, -1)
            self.send(h, f, s, sub, 1, 1 if sub == 0 else -1)
            self.send(h, f, s, sub, 1, -1 if sub == 0 else 1)
        else:
            if s == 3 and sub == 0:
                self.send(h, f, s, sub, 1, 1)
            if s == 1 and sub == 1:
                self.send(h, f, s, sub, 1, -1)

    def order(self):
        near = [(3, 0), (1, 1), (3, 1), (1, 0)]
        steps = [(a, 0, sub) for a, sub in near]
        steps += [(0, a, sub) for a, sub in near]
        steps += [(2, 0, 0), (2, 0, 1)]
        for f in (3, 1):
            steps += [(f, a, sub) for a, sub in near]
        steps += [(0, 2, 0), (0, 2, 1)]
        steps += [(2, a, sub) for a, sub in near]
        steps += [(f, 2, sub) for f in (3, 1, 2) for sub in range(2)]
        return [(h, *step) for step in steps for h in range(2)]

    def finish(self):
        for i in range(1, 4):
            self.share(i, False).wait_send()
        for copy in self.sent:
            copy.wait_send()


SPREAD_SEMS = [
    pltpu.SemaphoreType.DMA((4,)),
    pltpu.SemaphoreType.DMA((4,)),
    pltpu.SemaphoreType.DMA((60,)),
    pltpu.SemaphoreType.DMA((64,)),
]


def edge_exchange(right, left, right_all, left_all, s1s, s1r, rs, rr, l_send, l_recv, l_own):
    spread = Spread(right, right_all, s1s, s1r, rs, rr)
    x, zl, y, col = spread.x, spread.zl, spread.y, spread.col
    barrier = pltpu.get_barrier_semaphore()
    count = spread.greet(barrier)
    peers = [device(x, zl, y, col ^ 1), device(x, zl, y, col ^ 2), device(x, zl, y, col ^ 3)]
    for peer in peers:
        pl.semaphore_signal(barrier, inc=1, device_id=peer, device_id_type=MESH)
    pl.semaphore_wait(barrier, count + 3)
    spread.start()

    def left_copy(j, block):
        return pltpu.make_async_remote_copy(
            src_ref=left,
            dst_ref=left_all.at[block],
            send_sem=l_send.at[j],
            recv_sem=l_recv.at[j],
            device_id=peers[j],
            device_id_type=MESH,
        )

    for j in range(3):
        left_copy(j, col).start()
    own = pltpu.make_async_copy(left, left_all.at[col], l_own.at[0])
    own.start()
    spread.landed()
    spread.own()
    for step in spread.order():
        spread.take(*step)
    own.wait()
    for j in range(3):
        left_copy(j, col).wait_send()
        left_copy(j, col ^ (j + 1)).wait_recv()
    spread.finish()


def remote(src, dst, send, recv, to):
    return pltpu.make_async_remote_copy(
        src_ref=src, dst_ref=dst, send_sem=send, recv_sem=recv, device_id=to, device_id_type=MESH
    )


AHEAD = 8


def finish_kernel(
    bias, norm, mid, dead, att_in, att_out, new,
    bias_all, norm_all, bias_wide, s1s, s1r, rs, rr, sib, far_send, far_recv, fwd_send, fwd_recv,
):
    spread = Spread(bias, bias_all, s1s, s1r, rs, rr)
    x, zl, y, col = spread.x, spread.zl, spread.y, spread.col
    sibling = device(x, zl, y, col ^ 1)
    opposite = device(x, zl, y, col ^ 2)
    barrier = pltpu.get_barrier_semaphore()
    count = spread.greet(barrier)
    for peer in (sibling, opposite):
        pl.semaphore_signal(barrier, inc=1, device_id=peer, device_id_type=MESH)
    pl.semaphore_wait(barrier, count + 2)

    def far(r, block):
        return remote(norm.at[r], norm_all.at[block, r], far_send.at[r], far_recv.at[r], opposite)

    def forward(r, block):
        return remote(
            norm_all.at[col ^ 2, r], norm_all.at[block, r], fwd_send.at[r], fwd_recv.at[r], sibling
        )

    def near(block):
        return remote(norm, norm_all.at[block], sib.at[1], sib.at[2], sibling)

    def pass_on(r):
        far(r, col ^ 2).wait_recv()
        forward(r, col ^ 2).start()

    spread.start()
    for r in range(16):
        far(r, col).start()
    own = pltpu.make_async_copy(norm, norm_all.at[col], sib.at[0])
    own.start()
    near(col).start()
    spread.landed()
    spread.own()
    order = spread.order()
    for at, each in enumerate(order):
        spread.take(*each)
        if at % 6 == 5 and at // 6 < AHEAD:
            pass_on(at // 6)
    own.wait()
    near(col ^ 1).wait_recv()
    for h in range(H):
        for block in range(4):
            masked = dead[:, pl.ds(256 * block, 256)]
            for part in range(16):
                some = bias_all[h // 2, block, part % 4, part // 4, h % 2].astype(F32)
                bias_wide[h, pl.ds(16 * part, 16), pl.ds(256 * block, 256)] = some + masked
    lane_head = lax.broadcasted_iota(jnp.int32, (256, CH), 1) // DH
    ones = jnp.ones((1024, CH), BF16)

    def attend(r, carry):
        @pl.when(r < 16 - AHEAD)
        def _():
            pass_on(r + AHEAD)

        forward(r, col ^ 3).wait_recv()
        here = norm_all[:, r].reshape(4 * 256, CH)
        kv = jnp.dot(here, att_in[:, CH : 3 * CH], preferred_element_type=F32).astype(BF16)
        keys = kv[:, :CH]
        values = jnp.concatenate([kv[:, CH:], ones], axis=1)
        mine = norm[r]
        queries = jnp.dot(mine, att_in[:, :CH], preferred_element_type=F32).astype(BF16)
        gate = jax.nn.sigmoid(jnp.dot(mine, att_in[:, 3 * CH :], preferred_element_type=F32))
        attended = jnp.zeros((256, CH), F32)
        for h in range(H):
            query = jnp.where(lane_head == h, queries, jnp.zeros((), BF16))
            scores = lax.dot_general(
                query, keys, (((1,), (1,)), ((), ())), preferred_element_type=F32
            )
            scores = scores * (1.0 / math.sqrt(DH)) + bias_wide[h]
            top = jnp.max(scores, axis=-1, keepdims=True)
            weights = jnp.exp(scores - top).astype(BF16)
            summed = jnp.dot(weights, values, preferred_element_type=F32)
            attended = jnp.where(lane_head == h, summed[:, :CH] / summed[:, CH:], attended)
        attended = (attended * gate).astype(BF16)
        add = jnp.dot(attended, att_out[...], preferred_element_type=F32)
        new[r] = (mid[r].astype(F32) + add).astype(BF16)
        return carry

    lax.fori_loop(0, 16, attend, 0)
    near(col).wait_send()
    for r in range(16):
        far(r, col).wait_send()
        forward(r, col ^ 2).wait_send()
    spread.finish()


ANY = pl.BlockSpec(memory_space=pl.ANY)


def exchange_edges(right, left):
    return pl.pallas_call(
        edge_exchange,
        name="edge_exchange",
        out_shape=(
            jax.ShapeDtypeStruct((2, 4, 4, 4) + right.shape[1:], right.dtype),
            jax.ShapeDtypeStruct((4,) + left.shape, left.dtype),
        ),
        in_specs=[ANY, ANY],
        out_specs=(ANY, ANY),
        scratch_shapes=SPREAD_SEMS
        + [
            pltpu.SemaphoreType.DMA((3,)),
            pltpu.SemaphoreType.DMA((3,)),
            pltpu.SemaphoreType.DMA((1,)),
        ],
        compiler_params=pltpu.CompilerParams(collective_id=0, has_side_effects=True),
    )(right, left)


VM = pl.BlockSpec(memory_space=pltpu.VMEM)


def finish(bias, norm, mid, dead, att_in, att_out):
    return pl.pallas_call(
        finish_kernel,
        name="finish",
        out_shape=jax.ShapeDtypeStruct((16, 256, CH), BF16),
        in_specs=[VM] * 6,
        out_specs=VM,
        scratch_shapes=[
            pltpu.VMEM((2, 4, 4, 4) + bias.shape[1:], BF16),
            pltpu.VMEM((4,) + norm.shape, BF16),
            pltpu.VMEM((H, 256, 1024), F32),
        ]
        + SPREAD_SEMS
        + [pltpu.SemaphoreType.DMA((3,))]
        + [pltpu.SemaphoreType.DMA((16,))] * 4,
        compiler_params=pltpu.CompilerParams(
            collective_id=1, has_side_effects=True, vmem_limit_bytes=48 << 20
        ),
    )(bias, norm, mid, dead, att_in, att_out)


def triangle_kernel(
    right, left, pair, tri_gain, tri_in, sum_gain, tri_out, att_gain, att_bias,
    mid, norm, bias, left_wide, normed, bias_wide,
):
    at = pl.program_id(0)

    @pl.when(at == 0)
    def _():
        for b in range(4):
            left_wide[pl.ds(16 * b, 16)] = left[b].astype(F32)

    def contract(q, sums):
        block, half = q // 2, q % 2
        sums = list(sums)
        for k in range(8):
            edge = right[half, block, 0, 0, k].astype(F32)
            token = block * 16 + half * 8 + k
            for i in range(16):
                sums[i] = sums[i] + edge * left_wide[token, pl.ds(i, 1), :]
        return tuple(sums)

    zero = jnp.zeros((16, CH), F32)
    sums = lax.fori_loop(0, 8, contract, (zero,) * 16)
    for i in range(16):
        normed[i] = layer_norm(sums[i], sum_gain[...]).astype(BF16)
    update = jnp.dot(normed[...].reshape(256, CH), tri_out[...], preferred_element_type=F32)
    tile = pair[...].reshape(256, CH).astype(F32)
    tri_norm = layer_norm(tile, tri_gain[...]).astype(BF16)
    gate = jax.nn.sigmoid(jnp.dot(tri_norm, tri_in[...], preferred_element_type=F32))
    mid_tile = (tile + gate * update).astype(BF16)
    mid[...] = mid_tile.reshape(16, 16, CH)
    att = layer_norm(mid_tile, att_gain[...]).astype(BF16)
    norm[:, pl.ds(pl.multiple_of(at * 16, 16), 16), :] = att.reshape(16, 16, CH)

    @pl.when(at == 15)
    def _():
        for i in range(16):
            rows = lax.dot_general(
                att_bias[...], norm[i], (((1,), (1,)), ((), ())), preferred_element_type=F32
            )
            for h in range(H):
                bias_wide[h, pl.ds(i, 1), :] = rows[h : h + 1]
        for h in range(H):
            bias[h // 2, h % 2] = bias_wide[h].astype(BF16)


def triangle(right_all, left_all, pair_rep, tri_gain, tri_in, sum_gain, tri_out, att_gain, att_bias):
    whole = lambda *shape: pl.BlockSpec(shape, lambda t: (0,) * len(shape))
    bias_rows = jnp.zeros((8, CH), BF16).at[:H].set(att_bias.T)
    return pl.pallas_call(
        triangle_kernel,
        name="triangle",
        grid=(16,),
        out_shape=(
            jax.ShapeDtypeStruct((16, 256, CH), BF16),
            jax.ShapeDtypeStruct((16, 256, CH), BF16),
            jax.ShapeDtypeStruct((2, 2, 16, 256), BF16),
        ),
        in_specs=[
            pl.BlockSpec((2, 4, 1, 1, 8, 16, CH), lambda t: (0, 0, t % 4, t // 4, 0, 0, 0)),
            whole(4, 16, 16, CH),
            pl.BlockSpec((16, 16, CH), lambda t: (0, t, 0)),
            whole(1, CH),
            pl.BlockSpec((CH, CH), lambda t: (0, 4)),
            whole(1, CH),
            whole(CH, CH),
            whole(1, CH),
            whole(8, CH),
        ],
        out_specs=(
            pl.BlockSpec((16, 16, CH), lambda t: (0, t, 0)),
            whole(16, 256, CH),
            whole(2, 2, 16, 256),
        ),
        scratch_shapes=[
            pltpu.VMEM((64, 16, CH), F32),
            pltpu.VMEM((16, 16, CH), BF16),
            pltpu.VMEM((H, 16, 256), F32),
        ],
        compiler_params=pltpu.CompilerParams(vmem_limit_bytes=32 << 20),
    )(
        right_all, left_all, pair_rep, tri_gain.reshape(1, CH), tri_in, sum_gain.reshape(1, CH),
        tri_out, att_gain.reshape(1, CH), bias_rows,
    )


def body(
    pair_rep, chain_len, tri_gain, tri_in, sum_gain, tri_out, att_gain, att_in, att_bias, att_out
):
    row_count = pair_rep.shape[0]
    col_count = pair_rep.shape[1]
    live_all = live_tokens(chain_len)
    live_rows = lax.dynamic_slice_in_dim(live_all, lax.axis_index("row") * row_count, row_count)
    live_cols = lax.dynamic_slice_in_dim(live_all, lax.axis_index("col") * col_count, KCD)
    group_norm = layer_norm(pair_rep[:, :KCD], tri_gain).astype(BF16)
    group_proj = jnp.dot(group_norm, tri_in[:, : 4 * CH], preferred_element_type=F32)
    pair_live = live_rows[:, None, None] * live_cols[None, :, None]
    left_edge = (jax.nn.sigmoid(group_proj[..., :CH]) * group_proj[..., CH : 2 * CH] * pair_live).astype(BF16)
    right_edge = (
        jax.nn.sigmoid(group_proj[..., 2 * CH : 3 * CH]) * group_proj[..., 3 * CH :] * pair_live
    ).astype(BF16)
    left_edge = jnp.transpose(left_edge, (1, 0, 2))
    right_edge = jnp.transpose(right_edge, (1, 0, 2)).reshape(2, 8, 16, CH)
    right_all, left_all = exchange_edges(right_edge, left_edge)
    mid, norm, bias = triangle(
        right_all, left_all, pair_rep, tri_gain, tri_in, sum_gain, tri_out, att_gain, att_bias
    )
    dead = jnp.where(live_all > 0.5, 0.0, NEG_SCORE).reshape(1, -1)
    return finish(bias, norm, mid, dead, att_in, att_out)


def solution(mesh):
    placed = (P("row", "col", None), P(), P(), P(), P(), P(), P(), P(), P(), P())
    return jax.shard_map(
        body, mesh=mesh, in_specs=placed, out_specs=P("row", "col", None), check_vma=False
    )
```

```python
import math

import jax
import jax.numpy as jnp
from jax import lax
from jax.experimental import pallas as pl
from jax.experimental.pallas import tpu as pltpu
from jax.sharding import PartitionSpec as P

CH = 128
H = 4
DH = 32
KCD = 16
SLOT = 64
EPSILON = 1e-05
NEG_SCORE = -1e30
MESH = pl.DeviceIdType.MESH
F32 = jnp.float32
BF16 = jnp.bfloat16


def layer_norm(values, norm_gain):
    values = values.astype(F32)
    centre = values - jnp.mean(values, axis=-1, keepdims=True)
    spread = jnp.mean(centre * centre, axis=-1, keepdims=True)
    return centre * lax.rsqrt(spread + EPSILON) * norm_gain


def place():
    row = lax.axis_index("row")
    col = lax.axis_index("col")
    return row // 16, (row // 4) % 4, row % 4, col


def device(x, zl, y, col):
    return (x * 16 + zl * 4 + y, col)


class Spread:
    def __init__(self, pay, buf, s1_send, s1_recv, ring_send, ring_recv):
        self.pay, self.buf = pay, buf
        self.s1_send, self.s1_recv = s1_send, s1_recv
        self.ring_send, self.ring_recv = ring_send, ring_recv
        self.x, self.zl, self.y, self.col = place()
        self.swapped = self.x != self.col
        self.sent = []

    def partner(self):
        return device(self.col, self.zl, self.y, self.x)

    def line(self, i):
        return device(self.x, (self.zl + i) % 4, self.y, self.col)

    def neighbour(self, h, axis, d):
        along_y = (h == 0) == (axis == 0)
        if along_y:
            return device(self.x, self.zl, (self.y + d + 4) % 4, self.col)
        return device((self.x + d + 4) % 4, self.zl, self.y, self.col)

    def greet(self, barrier):
        def hello(to):
            pl.semaphore_signal(barrier, inc=1, device_id=to, device_id_type=MESH)

        for i in range(1, 4):
            hello(self.line(i))
        for axis in range(2):
            for d in (1, -1):
                hello(self.neighbour(0, axis, d))

        @pl.when(self.swapped)
        def _():
            hello(self.partner())

        return 7 + self.swapped.astype(jnp.int32)

    def swap(self, arrival):
        into = (self.x, self.zl) if arrival else (self.col, self.zl)
        return pltpu.make_async_remote_copy(
            src_ref=self.pay,
            dst_ref=self.buf.at[:, into[0], self.y, into[1]],
            send_sem=self.s1_send.at[0],
            recv_sem=self.s1_recv.at[0],
            device_id=self.partner(),
            device_id_type=MESH,
        )

    def keep(self):
        return pltpu.make_async_copy(
            self.pay, self.buf.at[:, self.x, self.y, self.zl], self.s1_send.at[0]
        )

    def share(self, i, arrival):
        block = self.buf.at[:, self.x, self.y, (self.zl + 4 - i) % 4 if arrival else self.zl]
        return pltpu.make_async_remote_copy(
            src_ref=block,
            dst_ref=block,
            send_sem=self.s1_send.at[i],
            recv_sem=self.s1_recv.at[i],
            device_id=self.line(i),
            device_id_type=MESH,
        )

    def start(self):
        @pl.when(self.swapped)
        def _():
            self.swap(False).start()

        @pl.when(jnp.logical_not(self.swapped))
        def _():
            self.keep().start()

    def landed(self):
        @pl.when(self.swapped)
        def _():
            self.swap(True).wait_recv()
            self.swap(False).wait_send()

        @pl.when(jnp.logical_not(self.swapped))
        def _():
            self.keep().wait()

        for i in (1, 3, 2):
            self.share(i, False).start()
        for i in (1, 3, 2):
            self.share(i, True).wait_recv()

    def piece(self, h, f, s, sub):
        xi, yi = (s, f) if h == 0 else (f, s)
        return self.buf.at[h, (self.x + xi) % 4, (self.y + yi) % 4, pl.ds(2 * sub, 2)]

    def slot(self, h, f, s, sub):
        return ((h * 4 + f) * 4 + s) * 2 + sub

    def send(self, h, f, s, sub, axis, d):
        there = ((f - d) % 4, s) if axis == 0 else (f, (s - d) % 4)
        copy = pltpu.make_async_remote_copy(
            src_ref=self.piece(h, f, s, sub),
            dst_ref=self.piece(h, f, s, sub),
            send_sem=self.ring_send.at[len(self.sent)],
            recv_sem=self.ring_recv.at[self.slot(h, *there, sub)],
            device_id=self.neighbour(h, axis, d),
            device_id_type=MESH,
        )
        copy.start()
        self.sent.append(copy)

    def own(self):
        for axis in range(2):
            for step in range(2):
                for h in range(2):
                    self.send(h, 0, 0, step, axis, 1)
                    self.send(h, 0, 0, 1 - step, axis, -1)

    def arrive(self, h, f, s, sub):
        pltpu.make_async_remote_copy(
            src_ref=self.piece(h, f, s, sub),
            dst_ref=self.piece(h, f, s, sub),
            send_sem=self.ring_send.at[0],
            recv_sem=self.ring_recv.at[self.slot(h, f, s, sub)],
            device_id=self.neighbour(h, 0, 1),
            device_id_type=MESH,
        ).wait_recv()

    def take(self, h, f, s, sub):
        self.arrive(h, f, s, sub)
        if s == 0:
            if f == 3 and sub == 0:
                self.send(h, f, s, sub, 0, 1)
            if f == 1 and sub == 1:
                self.send(h, f, s, sub, 0, -1)
            self.send(h, f, s, sub, 1, 1 if sub == 0 else -1)
            self.send(h, f, s, sub, 1, -1 if sub == 0 else 1)
        else:
            if s == 3 and sub == 0:
                self.send(h, f, s, sub, 1, 1)
            if s == 1 and sub == 1:
                self.send(h, f, s, sub, 1, -1)

    def order(self):
        near = [(3, 0), (1, 1), (3, 1), (1, 0)]
        steps = [(a, 0, sub) for a, sub in near]
        steps += [(0, a, sub) for a, sub in near]
        steps += [(2, 0, 0), (2, 0, 1)]
        for f in (3, 1):
            steps += [(f, a, sub) for a, sub in near]
        steps += [(0, 2, 0), (0, 2, 1)]
        steps += [(2, a, sub) for a, sub in near]
        steps += [(f, 2, sub) for f in (3, 1, 2) for sub in range(2)]
        return [(h, *step) for step in steps for h in range(2)]

    def finish(self):
        for i in range(1, 4):
            self.share(i, False).wait_send()
        for copy in self.sent:
            copy.wait_send()


SPREAD_SEMS = [
    pltpu.SemaphoreType.DMA((4,)),
    pltpu.SemaphoreType.DMA((4,)),
    pltpu.SemaphoreType.DMA((60,)),
    pltpu.SemaphoreType.DMA((64,)),
]


def remote(src, dst, send, recv, to):
    return pltpu.make_async_remote_copy(
        src_ref=src, dst_ref=dst, send_sem=send, recv_sem=recv, device_id=to, device_id_type=MESH
    )


AHEAD = 2


def sigmoid(v):
    return jax.nn.sigmoid(v)


def whole_kernel(
    chain_len, pair_hbm, tri_gain, tri_in, sum_gain, tri_out, att_gain, att_in, att_bias, att_out, new,
    pair, group, edges, left, right, right_all, left_all, left_wide, sums, gates, mid, norm,
    bias_rows, bias, bias_all, norm_all, bias_wide,
    a_s1s, a_s1r, a_rs, a_rr, left_send, left_recv, load,
    b_s1s, b_s1r, b_rs, b_rr, near_sem, far_send, far_recv, fwd_send, fwd_recv,
):
    first = Spread(right, right_all, a_s1s, a_s1r, a_rs, a_rr)
    second = Spread(bias, bias_all, b_s1s, b_s1r, b_rs, b_rr)
    x, zl, y, col = first.x, first.zl, first.y, first.col
    row = lax.axis_index("row")
    sibling = device(x, zl, y, col ^ 1)
    opposite = device(x, zl, y, col ^ 2)
    load_group = pltpu.make_async_copy(pair_hbm.at[:, pl.ds(0, KCD)], group, load.at[0])
    load_pair = pltpu.make_async_copy(pair_hbm, pair, load.at[1])
    load_group.start()
    load_pair.start()
    barrier = pltpu.get_barrier_semaphore()
    count = first.greet(barrier)
    for peer in (sibling, opposite):
        pl.semaphore_signal(barrier, inc=1, device_id=peer, device_id_type=MESH)

    load_group.wait()
    tri_norm = layer_norm(group[...].reshape(256, CH), tri_gain[...]).astype(BF16)
    proj = jnp.dot(tri_norm, tri_in[:, : 4 * CH], preferred_element_type=F32)
    cell = lax.broadcasted_iota(jnp.int32, (256, CH), 0)
    row_live = (row % 4) * 16 + cell // 16 < chain_len[row // 4]
    col_live = cell % 16 < chain_len[col * 4]
    live = jnp.where(row_live, 1.0, 0.0) * jnp.where(col_live, 1.0, 0.0)
    edges[0] = sigmoid(proj[:, :CH]) * proj[:, CH : 2 * CH] * live
    edges[1] = sigmoid(proj[:, 2 * CH : 3 * CH]) * proj[:, 3 * CH :] * live
    for k in range(16):
        left[k] = edges[0, pl.ds(k, 16, stride=16), :].astype(BF16)
        right[k // 8, k % 8] = edges[1, pl.ds(k, 16, stride=16), :].astype(BF16)

    pl.semaphore_wait(barrier, count + 2)
    first.start()
    left_near = remote(left, left_all.at[col], left_send.at[0], left_recv.at[0], sibling)
    left_far = remote(left, left_all.at[col], left_send.at[1], left_recv.at[1], opposite)
    left_near.start()
    left_far.start()
    load_pair.wait()

    def prepare(i, carry):
        normed = layer_norm(pair[i], tri_gain[...]).astype(BF16)
        gates[i] = sigmoid(jnp.dot(normed, tri_in[:, 4 * CH :], preferred_element_type=F32))
        sums[i] = jnp.zeros((16, 16, CH), F32)
        return carry

    lax.fori_loop(0, 16, prepare, 0)
    first.landed()
    first.own()

    def left_forward(block):
        return remote(
            left_all.at[col ^ 2], left_all.at[block], left_send.at[2], left_recv.at[2], sibling
        )

    remote(left, left_all.at[col ^ 2], left_send.at[1], left_recv.at[1], opposite).wait_recv()
    left_forward(col ^ 2).start()
    remote(left, left_all.at[col ^ 1], left_send.at[0], left_recv.at[0], sibling).wait_recv()
    left_wide[pl.ds(16 * col, 16)] = left[...].astype(F32)
    for j in (1, 2):
        left_wide[pl.ds(16 * (col ^ j), 16)] = left_all[col ^ j].astype(F32)
    left_forward(col ^ 3).wait_recv()
    left_wide[pl.ds(16 * (col ^ 3), 16)] = left_all[col ^ 3].astype(F32)

    def contract(h, f, s):
        xi, yi = (s, f) if h == 0 else (f, s)
        xi, yi = (x + xi) % 4, (y + yi) % 4

        def tile(z, carry):
            part = z * 4 + yi

            def tokens(q, total):
                total = list(total)
                for u in range(2):
                    k = 2 * q + u
                    edge = right_all[h, xi, yi, z, k].astype(F32)
                    for i in range(16):
                        total[i] = total[i] + edge * left_wide[xi * 16 + h * 8 + k, pl.ds(i, 1), :]
                return tuple(total)

            total = lax.fori_loop(0, 4, tokens, tuple(sums[i, part] for i in range(16)))
            for i in range(16):
                sums[i, part] = total[i]
            return carry

        lax.fori_loop(0, 4, tile, 0)

    contract(0, 0, 0)
    contract(1, 0, 0)
    seen = {}
    for h, f, s, sub in first.order():
        first.take(h, f, s, sub)
        seen[(h, f, s)] = seen.get((h, f, s), 0) + 1
        if seen[(h, f, s)] == 2:
            contract(h, f, s)
    first.finish()
    left_near.wait_send()
    left_far.wait_send()
    left_forward(col ^ 2).wait_send()

    def close(i, carry):
        sum_norm = layer_norm(sums[i].reshape(256, CH), sum_gain[...]).astype(BF16)
        update = jnp.dot(sum_norm, tri_out[...], preferred_element_type=F32)
        mid_row = (pair[i].astype(F32) + gates[i] * update).astype(BF16)
        mid[i] = mid_row
        att = layer_norm(mid_row, att_gain[...]).astype(BF16)
        norm[i] = att
        norm_all[col, i] = att
        rows = lax.dot_general(att_bias[...], att, (((1,), (1,)), ((), ())), preferred_element_type=F32)
        for h in range(H):
            bias_rows[h, pl.ds(i, 1), :] = rows[h : h + 1]
        return carry

    lax.fori_loop(0, 16, close, 0)
    for h in range(H):
        bias[h // 2, h % 2] = bias_rows[h].astype(BF16)
    second.start()

    def far(r, block):
        return remote(norm.at[r], norm_all.at[block, r], far_send.at[r], far_recv.at[r], opposite)

    def forward(r, block):
        return remote(
            norm_all.at[col ^ 2, r], norm_all.at[block, r], fwd_send.at[r], fwd_recv.at[r], sibling
        )

    def near(block):
        return remote(norm, norm_all.at[block], near_sem.at[0], near_sem.at[1], sibling)

    def pass_on(r):
        far(r, col ^ 2).wait_recv()
        forward(r, col ^ 2).start()

    near(col).start()
    second.landed()
    second.own()
    for r in range(16):
        far(r, col).start()
    for each in second.order():
        second.take(*each)
    for r in range(AHEAD):
        pass_on(r)
    near(col ^ 1).wait_recv()
    lane = lax.broadcasted_iota(jnp.int32, (16, 256), 1)
    for block in range(4):
        length = jnp.zeros((16, 256), jnp.int32)
        for c in range(4):
            length = jnp.where(lane // SLOT == c, chain_len[block * 4 + c], length)
        masked = jnp.where(lane % SLOT < length, 0.0, NEG_SCORE)
        for h in range(H):
            for part in range(16):
                some = bias_all[h // 2, block, part % 4, part // 4, h % 2].astype(F32)
                bias_wide[h, pl.ds(16 * part, 16), pl.ds(256 * block, 256)] = some + masked
    lane_head = lax.broadcasted_iota(jnp.int32, (256, CH), 1) // DH
    ones = jnp.ones((1024, CH), BF16)

    def attend(r, carry):
        @pl.when(r < 16 - AHEAD)
        def _():
            pass_on(r + AHEAD)

        forward(r, col ^ 3).wait_recv()
        here = norm_all[:, r].reshape(4 * 256, CH)
        kv = jnp.dot(here, att_in[:, CH : 3 * CH], preferred_element_type=F32).astype(BF16)
        keys = kv[:, :CH]
        values = jnp.concatenate([kv[:, CH:], ones], axis=1)
        mine = norm[r]
        queries = jnp.dot(mine, att_in[:, :CH], preferred_element_type=F32).astype(BF16)
        gate = jax.nn.sigmoid(jnp.dot(mine, att_in[:, 3 * CH :], preferred_element_type=F32))
        attended = jnp.zeros((256, CH), F32)
        for h in range(H):
            query = jnp.where(lane_head == h, queries, jnp.zeros((), BF16))
            scores = lax.dot_general(
                query, keys, (((1,), (1,)), ((), ())), preferred_element_type=F32
            )
            scores = scores * (1.0 / math.sqrt(DH)) + bias_wide[h]
            top = jnp.max(scores, axis=-1, keepdims=True)
            weights = jnp.exp(scores - top).astype(BF16)
            summed = jnp.dot(weights, values, preferred_element_type=F32)
            attended = jnp.where(lane_head == h, summed[:, :CH] / summed[:, CH:], attended)
        attended = (attended * gate).astype(BF16)
        add = jnp.dot(attended, att_out[...], preferred_element_type=F32)
        new[r] = (mid[r].astype(F32) + add).astype(BF16)
        return carry

    lax.fori_loop(0, 16, attend, 0)
    near(col).wait_send()
    for r in range(16):
        far(r, col).wait_send()
        forward(r, col ^ 2).wait_send()
    second.finish()


ANY = pl.BlockSpec(memory_space=pl.ANY)
VM = pl.BlockSpec(memory_space=pltpu.VMEM)
SM = pl.BlockSpec(memory_space=pltpu.SMEM)


def body(
    pair_rep, chain_len, tri_gain, tri_in, sum_gain, tri_out, att_gain, att_in, att_bias, att_out
):
    bias_rows = jnp.pad(att_bias.T, ((0, 8 - H), (0, 0)))
    vmem = pltpu.VMEM
    return pl.pallas_call(
        whole_kernel,
        name="whole",
        out_shape=jax.ShapeDtypeStruct((16, 256, CH), BF16),
        in_specs=[SM, ANY] + [VM] * 8,
        out_specs=VM,
        scratch_shapes=[
            vmem((16, 256, CH), BF16),
            vmem((16, KCD, CH), BF16),
            vmem((2, 256, CH), F32),
            vmem((16, 16, CH), BF16),
            vmem((2, 8, 16, CH), BF16),
            vmem((2, 4, 4, 4, 8, 16, CH), BF16),
            vmem((4, 16, 16, CH), BF16),
            vmem((64, 16, CH), F32),
            vmem((16, 16, 16, CH), F32),
            vmem((16, 256, CH), F32),
            vmem((16, 256, CH), BF16),
            vmem((16, 256, CH), BF16),
            vmem((H, 16, 256), F32),
            vmem((2, 2, 16, 256), BF16),
            vmem((2, 4, 4, 4, 2, 16, 256), BF16),
            vmem((4, 16, 256, CH), BF16),
            vmem((H, 256, 1024), F32),
        ]
        + SPREAD_SEMS
        + [pltpu.SemaphoreType.DMA((3,)), pltpu.SemaphoreType.DMA((3,)), pltpu.SemaphoreType.DMA((2,))]
        + SPREAD_SEMS
        + [pltpu.SemaphoreType.DMA((2,))]
        + [pltpu.SemaphoreType.DMA((16,))] * 4,
        compiler_params=pltpu.CompilerParams(
            collective_id=0, has_side_effects=True, vmem_limit_bytes=56 << 20
        ),
    )(
        chain_len, pair_rep, tri_gain.reshape(1, CH), tri_in, sum_gain.reshape(1, CH), tri_out,
        att_gain.reshape(1, CH), att_in, bias_rows, att_out,
    )


def solution(mesh):
    placed = (P("row", "col", None), P(), P(), P(), P(), P(), P(), P(), P(), P())
    return jax.shard_map(
        body, mesh=mesh, in_specs=placed, out_specs=P("row", "col", None), check_vma=False
    )
```

```python
import math

import jax
import jax.numpy as jnp
from jax import lax
from jax.experimental import pallas as pl
from jax.experimental.pallas import tpu as pltpu
from jax.sharding import PartitionSpec as P

CH = 128
H = 4
DH = 32
KCD = 16
SLOT = 64
EPSILON = 1e-05
NEG_SCORE = -1e30
MESH = pl.DeviceIdType.MESH
F32 = jnp.float32
BF16 = jnp.bfloat16


def layer_norm(values, norm_gain):
    values = values.astype(F32)
    centre = values - jnp.mean(values, axis=-1, keepdims=True)
    spread = jnp.mean(centre * centre, axis=-1, keepdims=True)
    return centre * lax.rsqrt(spread + EPSILON) * norm_gain


def place():
    row = lax.axis_index("row")
    col = lax.axis_index("col")
    return row // 16, (row // 4) % 4, row % 4, col


def device(x, zl, y, col):
    return (x * 16 + zl * 4 + y, col)


class Spread:
    def __init__(self, pay, buf, s1_send, s1_recv, ring_send, ring_recv):
        self.pay, self.buf = pay, buf
        self.s1_send, self.s1_recv = s1_send, s1_recv
        self.ring_send, self.ring_recv = ring_send, ring_recv
        self.x, self.zl, self.y, self.col = place()
        self.swapped = self.x != self.col
        self.sent = []

    def partner(self):
        return device(self.col, self.zl, self.y, self.x)

    def line(self, i):
        return device(self.x, (self.zl + i) % 4, self.y, self.col)

    def neighbour(self, h, axis, d):
        along_y = (h == 0) == (axis == 0)
        if along_y:
            return device(self.x, self.zl, (self.y + d + 4) % 4, self.col)
        return device((self.x + d + 4) % 4, self.zl, self.y, self.col)

    def greet(self, barrier):
        def hello(to):
            pl.semaphore_signal(barrier, inc=1, device_id=to, device_id_type=MESH)

        for i in range(1, 4):
            hello(self.line(i))
        for axis in range(2):
            for d in (1, -1):
                hello(self.neighbour(0, axis, d))

        @pl.when(self.swapped)
        def _():
            hello(self.partner())

        return 7 + self.swapped.astype(jnp.int32)

    def swap(self, arrival):
        into = (self.x, self.zl) if arrival else (self.col, self.zl)
        return pltpu.make_async_remote_copy(
            src_ref=self.pay,
            dst_ref=self.buf.at[:, into[0], self.y, into[1]],
            send_sem=self.s1_send.at[0],
            recv_sem=self.s1_recv.at[0],
            device_id=self.partner(),
            device_id_type=MESH,
        )

    def keep(self):
        return pltpu.make_async_copy(
            self.pay, self.buf.at[:, self.x, self.y, self.zl], self.s1_send.at[0]
        )

    def share(self, i, arrival):
        block = self.buf.at[:, self.x, self.y, (self.zl + 4 - i) % 4 if arrival else self.zl]
        return pltpu.make_async_remote_copy(
            src_ref=block,
            dst_ref=block,
            send_sem=self.s1_send.at[i],
            recv_sem=self.s1_recv.at[i],
            device_id=self.line(i),
            device_id_type=MESH,
        )

    def start(self):
        @pl.when(self.swapped)
        def _():
            self.swap(False).start()

        @pl.when(jnp.logical_not(self.swapped))
        def _():
            self.keep().start()

    def landed(self):
        @pl.when(self.swapped)
        def _():
            self.swap(True).wait_recv()
            self.swap(False).wait_send()

        @pl.when(jnp.logical_not(self.swapped))
        def _():
            self.keep().wait()

        for i in (1, 3, 2):
            self.share(i, False).start()
        for i in (1, 3, 2):
            self.share(i, True).wait_recv()

    def piece(self, h, f, s, sub):
        xi, yi = (s, f) if h == 0 else (f, s)
        return self.buf.at[h, (self.x + xi) % 4, (self.y + yi) % 4, pl.ds(2 * sub, 2)]

    def slot(self, h, f, s, sub):
        return ((h * 4 + f) * 4 + s) * 2 + sub

    def send(self, h, f, s, sub, axis, d):
        there = ((f - d) % 4, s) if axis == 0 else (f, (s - d) % 4)
        copy = pltpu.make_async_remote_copy(
            src_ref=self.piece(h, f, s, sub),
            dst_ref=self.piece(h, f, s, sub),
            send_sem=self.ring_send.at[len(self.sent)],
            recv_sem=self.ring_recv.at[self.slot(h, *there, sub)],
            device_id=self.neighbour(h, axis, d),
            device_id_type=MESH,
        )
        copy.start()
        self.sent.append(copy)

    def own(self):
        for axis in range(2):
            for step in range(2):
                for h in range(2):
                    self.send(h, 0, 0, step, axis, 1)
                    self.send(h, 0, 0, 1 - step, axis, -1)

    def arrive(self, h, f, s, sub):
        pltpu.make_async_remote_copy(
            src_ref=self.piece(h, f, s, sub),
            dst_ref=self.piece(h, f, s, sub),
            send_sem=self.ring_send.at[0],
            recv_sem=self.ring_recv.at[self.slot(h, f, s, sub)],
            device_id=self.neighbour(h, 0, 1),
            device_id_type=MESH,
        ).wait_recv()

    def take(self, h, f, s, sub):
        self.arrive(h, f, s, sub)
        if s == 0:
            if f == 3 and sub == 0:
                self.send(h, f, s, sub, 0, 1)
            if f == 1 and sub == 1:
                self.send(h, f, s, sub, 0, -1)
            self.send(h, f, s, sub, 1, 1 if sub == 0 else -1)
            self.send(h, f, s, sub, 1, -1 if sub == 0 else 1)
        else:
            if s == 3 and sub == 0:
                self.send(h, f, s, sub, 1, 1)
            if s == 1 and sub == 1:
                self.send(h, f, s, sub, 1, -1)

    def order(self):
        near = [(3, 0), (1, 1), (3, 1), (1, 0)]
        steps = [(a, 0, sub) for a, sub in near]
        steps += [(0, a, sub) for a, sub in near]
        steps += [(2, 0, 0), (2, 0, 1)]
        for f in (3, 1):
            steps += [(f, a, sub) for a, sub in near]
        steps += [(0, 2, 0), (0, 2, 1)]
        steps += [(2, a, sub) for a, sub in near]
        steps += [(f, 2, sub) for f in (3, 1, 2) for sub in range(2)]
        return [(h, *step) for step in steps for h in range(2)]

    def finish(self):
        for i in range(1, 4):
            self.share(i, False).wait_send()
        for copy in self.sent:
            copy.wait_send()


SPREAD_SEMS = [
    pltpu.SemaphoreType.DMA((4,)),
    pltpu.SemaphoreType.DMA((4,)),
    pltpu.SemaphoreType.DMA((60,)),
    pltpu.SemaphoreType.DMA((64,)),
]


def remote(src, dst, send, recv, to):
    return pltpu.make_async_remote_copy(
        src_ref=src, dst_ref=dst, send_sem=send, recv_sem=recv, device_id=to, device_id_type=MESH
    )


AHEAD = 2
EARLY = 4
FAR_AT = 4


def sigmoid(v):
    return jax.nn.sigmoid(v)


def whole_kernel(
    chain_len, pair_hbm, tri_gain, tri_in, sum_gain, tri_out, att_gain, att_in, att_bias, att_out, new,
    pair, group, edges, left, right, right_all, left_all, left_wide, sums, gates, mid, norm,
    bias_rows, bias, bias_all, norm_all, bias_wide,
    a_s1s, a_s1r, a_rs, a_rr, left_send, left_recv, load,
    b_s1s, b_s1r, b_rs, b_rr, near_sem, far_send, far_recv, fwd_send, fwd_recv,
):
    first = Spread(right, right_all, a_s1s, a_s1r, a_rs, a_rr)
    second = Spread(bias, bias_all, b_s1s, b_s1r, b_rs, b_rr)
    x, zl, y, col = first.x, first.zl, first.y, first.col
    row = lax.axis_index("row")
    sibling = device(x, zl, y, col ^ 1)
    opposite = device(x, zl, y, col ^ 2)
    load_group = pltpu.make_async_copy(pair_hbm.at[:, pl.ds(0, KCD)], group, load.at[0])
    load_pair = pltpu.make_async_copy(pair_hbm, pair, load.at[1])
    load_group.start()
    load_pair.start()
    barrier = pltpu.get_barrier_semaphore()
    count = first.greet(barrier)
    for peer in (sibling, opposite):
        pl.semaphore_signal(barrier, inc=1, device_id=peer, device_id_type=MESH)

    load_group.wait()
    tri_norm = layer_norm(group[...].reshape(256, CH), tri_gain[...]).astype(BF16)
    proj = jnp.dot(tri_norm, tri_in[:, : 4 * CH], preferred_element_type=F32)
    cell = lax.broadcasted_iota(jnp.int32, (256, CH), 0)
    row_live = (row % 4) * 16 + cell // 16 < chain_len[row // 4]
    col_live = cell % 16 < chain_len[col * 4]
    live = jnp.where(row_live, 1.0, 0.0) * jnp.where(col_live, 1.0, 0.0)
    edges[0] = sigmoid(proj[:, :CH]) * proj[:, CH : 2 * CH] * live
    edges[1] = sigmoid(proj[:, 2 * CH : 3 * CH]) * proj[:, 3 * CH :] * live
    for k in range(16):
        left[k] = edges[0, pl.ds(k, 16, stride=16), :].astype(BF16)
        right[k // 8, k % 8] = edges[1, pl.ds(k, 16, stride=16), :].astype(BF16)

    pl.semaphore_wait(barrier, count + 2)
    first.start()
    left_near = remote(left, left_all.at[col], left_send.at[0], left_recv.at[0], sibling)
    left_far = remote(left, left_all.at[col], left_send.at[1], left_recv.at[1], opposite)
    left_near.start()
    left_far.start()
    load_pair.wait()

    def prepare(i, carry):
        normed = layer_norm(pair[i], tri_gain[...]).astype(BF16)
        gates[i] = sigmoid(jnp.dot(normed, tri_in[:, 4 * CH :], preferred_element_type=F32))
        sums[i] = jnp.zeros((16, 16, CH), F32)
        return carry

    lax.fori_loop(0, 16, prepare, 0)
    first.landed()
    first.own()

    def left_forward(block):
        return remote(
            left_all.at[col ^ 2], left_all.at[block], left_send.at[2], left_recv.at[2], sibling
        )

    remote(left, left_all.at[col ^ 2], left_send.at[1], left_recv.at[1], opposite).wait_recv()
    left_forward(col ^ 2).start()
    remote(left, left_all.at[col ^ 1], left_send.at[0], left_recv.at[0], sibling).wait_recv()
    left_wide[pl.ds(16 * col, 16)] = left[...].astype(F32)
    for j in (1, 2):
        left_wide[pl.ds(16 * (col ^ j), 16)] = left_all[col ^ j].astype(F32)
    left_forward(col ^ 3).wait_recv()
    left_wide[pl.ds(16 * (col ^ 3), 16)] = left_all[col ^ 3].astype(F32)

    def contract(h, f, s):
        xi, yi = (s, f) if h == 0 else (f, s)
        xi, yi = (x + xi) % 4, (y + yi) % 4

        def tile(z, carry):
            part = z * 4 + yi

            def tokens(q, total):
                total = list(total)
                for u in range(2):
                    k = 2 * q + u
                    edge = right_all[h, xi, yi, z, k].astype(F32)
                    for i in range(16):
                        total[i] = total[i] + edge * left_wide[xi * 16 + h * 8 + k, pl.ds(i, 1), :]
                return tuple(total)

            total = lax.fori_loop(0, 4, tokens, tuple(sums[i, part] for i in range(16)))
            for i in range(16):
                sums[i, part] = total[i]
            return carry

        lax.fori_loop(0, 4, tile, 0)

    contract(0, 0, 0)
    contract(1, 0, 0)
    seen = {}
    for h, f, s, sub in first.order():
        first.take(h, f, s, sub)
        seen[(h, f, s)] = seen.get((h, f, s), 0) + 1
        if seen[(h, f, s)] == 2:
            contract(h, f, s)
    first.finish()
    left_near.wait_send()
    left_far.wait_send()
    left_forward(col ^ 2).wait_send()

    def far(r, block):
        return remote(norm.at[r], norm_all.at[block, r], far_send.at[r], far_recv.at[r], opposite)

    def close_row(i):
        sum_norm = layer_norm(sums[i].reshape(256, CH), sum_gain[...]).astype(BF16)
        update = jnp.dot(sum_norm, tri_out[...], preferred_element_type=F32)
        mid_row = (pair[i].astype(F32) + gates[i] * update).astype(BF16)
        mid[i] = mid_row
        att = layer_norm(mid_row, att_gain[...]).astype(BF16)
        norm[i] = att
        norm_all[col, i] = att
        rows = lax.dot_general(att_bias[...], att, (((1,), (1,)), ((), ())), preferred_element_type=F32)
        for h in range(H):
            bias_rows[h, pl.ds(i, 1), :] = rows[h : h + 1]

    def close(i, carry):
        close_row(2 * i)
        close_row(2 * i + 1)

        @pl.when(i < EARLY // 2)
        def _():
            far(2 * i, col).start()
            far(2 * i + 1, col).start()

        return carry

    lax.fori_loop(0, 8, close, 0)
    for h in range(H):
        bias[h // 2, h % 2] = bias_rows[h].astype(BF16)
    second.start()

    def forward(r, block):
        return remote(
            norm_all.at[col ^ 2, r], norm_all.at[block, r], fwd_send.at[r], fwd_recv.at[r], sibling
        )

    def near(block):
        return remote(norm, norm_all.at[block], near_sem.at[0], near_sem.at[1], sibling)

    def pass_on(r):
        far(r, col ^ 2).wait_recv()
        forward(r, col ^ 2).start()

    near(col).start()
    second.landed()
    second.own()

    def far_rest():
        for r in range(EARLY, 16):
            far(r, col).start()

    z_here = (col // 2) * 4 + zl
    pl.when(z_here == 0)(far_rest)
    for at, each in enumerate(second.order()):
        second.take(*each)
        if at == FAR_AT:
            pl.when(z_here != 0)(far_rest)
    for r in range(AHEAD):
        pass_on(r)
    near(col ^ 1).wait_recv()
    lane = lax.broadcasted_iota(jnp.int32, (16, 256), 1)
    for block in range(4):
        length = jnp.zeros((16, 256), jnp.int32)
        for c in range(4):
            length = jnp.where(lane // SLOT == c, chain_len[block * 4 + c], length)
        masked = jnp.where(lane % SLOT < length, 0.0, NEG_SCORE)
        for h in range(H):
            for part in range(16):
                some = bias_all[h // 2, block, part % 4, part // 4, h % 2].astype(F32)
                bias_wide[h, pl.ds(16 * part, 16), pl.ds(256 * block, 256)] = some + masked
    lane_head = lax.broadcasted_iota(jnp.int32, (256, CH), 1) // DH
    ones = jnp.ones((1024, CH), BF16)

    def attend_row(r):
        here = norm_all[:, r].reshape(4 * 256, CH)
        kv = jnp.dot(here, att_in[:, CH : 3 * CH], preferred_element_type=F32).astype(BF16)
        keys = kv[:, :CH]
        values = jnp.concatenate([kv[:, CH:], ones], axis=1)
        mine = norm[r]
        queries = jnp.dot(mine, att_in[:, :CH], preferred_element_type=F32).astype(BF16)
        gate = jax.nn.sigmoid(jnp.dot(mine, att_in[:, 3 * CH :], preferred_element_type=F32))
        attended = jnp.zeros((256, CH), F32)
        for h in range(H):
            query = jnp.where(lane_head == h, queries, jnp.zeros((), BF16))
            scores = lax.dot_general(
                query, keys, (((1,), (1,)), ((), ())), preferred_element_type=F32
            )
            scores = scores * (1.0 / math.sqrt(DH)) + bias_wide[h]
            top = jnp.max(scores, axis=-1, keepdims=True)
            weights = jnp.exp(scores - top).astype(BF16)
            summed = jnp.dot(weights, values, preferred_element_type=F32)
            attended = jnp.where(lane_head == h, summed[:, :CH] / summed[:, CH:], attended)
        attended = (attended * gate).astype(BF16)
        add = jnp.dot(attended, att_out[...], preferred_element_type=F32)
        new[r] = (mid[r].astype(F32) + add).astype(BF16)

    def attend(q, carry):
        @pl.when(q < 7)
        def _():
            pass_on(2 * q + 2)
            pass_on(2 * q + 3)

        forward(2 * q, col ^ 3).wait_recv()
        forward(2 * q + 1, col ^ 3).wait_recv()
        attend_row(2 * q)
        attend_row(2 * q + 1)
        return carry

    lax.fori_loop(0, 8, attend, 0)
    near(col).wait_send()
    for r in range(16):
        far(r, col).wait_send()
        forward(r, col ^ 2).wait_send()
    second.finish()


ANY = pl.BlockSpec(memory_space=pl.ANY)
VM = pl.BlockSpec(memory_space=pltpu.VMEM)
SM = pl.BlockSpec(memory_space=pltpu.SMEM)


def body(
    pair_rep, chain_len, tri_gain, tri_in, sum_gain, tri_out, att_gain, att_in, att_bias, att_out
):
    bias_rows = jnp.pad(att_bias.T, ((0, 8 - H), (0, 0)))
    vmem = pltpu.VMEM
    return pl.pallas_call(
        whole_kernel,
        name="whole",
        out_shape=jax.ShapeDtypeStruct((16, 256, CH), BF16),
        in_specs=[SM, ANY] + [VM] * 8,
        out_specs=VM,
        scratch_shapes=[
            vmem((16, 256, CH), BF16),
            vmem((16, KCD, CH), BF16),
            vmem((2, 256, CH), F32),
            vmem((16, 16, CH), BF16),
            vmem((2, 8, 16, CH), BF16),
            vmem((2, 4, 4, 4, 8, 16, CH), BF16),
            vmem((4, 16, 16, CH), BF16),
            vmem((64, 16, CH), F32),
            vmem((16, 16, 16, CH), F32),
            vmem((16, 256, CH), F32),
            vmem((16, 256, CH), BF16),
            vmem((16, 256, CH), BF16),
            vmem((H, 16, 256), F32),
            vmem((2, 2, 16, 256), BF16),
            vmem((2, 4, 4, 4, 2, 16, 256), BF16),
            vmem((4, 16, 256, CH), BF16),
            vmem((H, 256, 1024), F32),
        ]
        + SPREAD_SEMS
        + [pltpu.SemaphoreType.DMA((3,)), pltpu.SemaphoreType.DMA((3,)), pltpu.SemaphoreType.DMA((2,))]
        + SPREAD_SEMS
        + [pltpu.SemaphoreType.DMA((2,))]
        + [pltpu.SemaphoreType.DMA((16,))] * 4,
        compiler_params=pltpu.CompilerParams(
            collective_id=0, has_side_effects=True, vmem_limit_bytes=56 << 20
        ),
    )(
        chain_len, pair_rep, tri_gain.reshape(1, CH), tri_in, sum_gain.reshape(1, CH), tri_out,
        att_gain.reshape(1, CH), att_in, bias_rows, att_out,
    )


def solution(mesh):
    placed = (P("row", "col", None), P(), P(), P(), P(), P(), P(), P(), P(), P())
    return jax.shard_map(
        body, mesh=mesh, in_specs=placed, out_specs=P("row", "col", None), check_vma=False
    )
```

```python
import math

import jax
import jax.numpy as jnp
from jax import lax
from jax.experimental import pallas as pl
from jax.experimental.pallas import tpu as pltpu
from jax.sharding import PartitionSpec as P

CH = 128
H = 4
DH = 32
KCD = 16
SLOT = 64
EPSILON = 1e-05
NEG_SCORE = -1e30
MESH = pl.DeviceIdType.MESH
F32 = jnp.float32
BF16 = jnp.bfloat16


def layer_norm(values, norm_gain):
    values = values.astype(F32)
    centre = values - jnp.mean(values, axis=-1, keepdims=True)
    spread = jnp.mean(centre * centre, axis=-1, keepdims=True)
    return centre * lax.rsqrt(spread + EPSILON) * norm_gain


def place():
    row = lax.axis_index("row")
    col = lax.axis_index("col")
    return row // 16, (row // 4) % 4, row % 4, col


def device(x, zl, y, col):
    return (x * 16 + zl * 4 + y, col)


class Spread:
    def __init__(self, pay, buf, s1_send, s1_recv, ring_send, ring_recv):
        self.pay, self.buf = pay, buf
        self.s1_send, self.s1_recv = s1_send, s1_recv
        self.ring_send, self.ring_recv = ring_send, ring_recv
        self.x, self.zl, self.y, self.col = place()
        self.swapped = self.x != self.col
        self.sent = []

    def partner(self):
        return device(self.col, self.zl, self.y, self.x)

    def line(self, i):
        return device(self.x, (self.zl + i) % 4, self.y, self.col)

    def neighbour(self, h, axis, d):
        along_y = (h == 0) == (axis == 0)
        if along_y:
            return device(self.x, self.zl, (self.y + d + 4) % 4, self.col)
        return device((self.x + d + 4) % 4, self.zl, self.y, self.col)

    def greet(self, barrier):
        def hello(to):
            pl.semaphore_signal(barrier, inc=1, device_id=to, device_id_type=MESH)

        for i in range(1, 4):
            hello(self.line(i))
        for axis in range(2):
            for d in (1, -1):
                hello(self.neighbour(0, axis, d))

        @pl.when(self.swapped)
        def _():
            hello(self.partner())

        return 7 + self.swapped.astype(jnp.int32)

    def swap(self, arrival):
        into = (self.x, self.zl) if arrival else (self.col, self.zl)
        return pltpu.make_async_remote_copy(
            src_ref=self.pay,
            dst_ref=self.buf.at[:, into[0], self.y, into[1]],
            send_sem=self.s1_send.at[0],
            recv_sem=self.s1_recv.at[0],
            device_id=self.partner(),
            device_id_type=MESH,
        )

    def keep(self):
        return pltpu.make_async_copy(
            self.pay, self.buf.at[:, self.x, self.y, self.zl], self.s1_send.at[0]
        )

    def share(self, i, arrival):
        block = self.buf.at[:, self.x, self.y, (self.zl + 4 - i) % 4 if arrival else self.zl]
        return pltpu.make_async_remote_copy(
            src_ref=block,
            dst_ref=block,
            send_sem=self.s1_send.at[i],
            recv_sem=self.s1_recv.at[i],
            device_id=self.line(i),
            device_id_type=MESH,
        )

    def start(self):
        @pl.when(self.swapped)
        def _():
            self.swap(False).start()

        @pl.when(jnp.logical_not(self.swapped))
        def _():
            self.keep().start()

    def landed(self, during=None):
        @pl.when(self.swapped)
        def _():
            self.swap(True).wait_recv()
            self.swap(False).wait_send()

        @pl.when(jnp.logical_not(self.swapped))
        def _():
            self.keep().wait()

        for i in (1, 3, 2):
            self.share(i, False).start()
        if during is not None:
            during()
        for i in (1, 3, 2):
            self.share(i, True).wait_recv()

    def piece(self, h, f, s, sub):
        xi, yi = (s, f) if h == 0 else (f, s)
        return self.buf.at[h, (self.x + xi) % 4, (self.y + yi) % 4, pl.ds(2 * sub, 2)]

    def slot(self, h, f, s, sub):
        return ((h * 4 + f) * 4 + s) * 2 + sub

    def send(self, h, f, s, sub, axis, d):
        there = ((f - d) % 4, s) if axis == 0 else (f, (s - d) % 4)
        copy = pltpu.make_async_remote_copy(
            src_ref=self.piece(h, f, s, sub),
            dst_ref=self.piece(h, f, s, sub),
            send_sem=self.ring_send.at[len(self.sent)],
            recv_sem=self.ring_recv.at[self.slot(h, *there, sub)],
            device_id=self.neighbour(h, axis, d),
            device_id_type=MESH,
        )
        copy.start()
        self.sent.append(copy)

    def own(self):
        for axis in range(2):
            for step in range(2):
                for h in range(2):
                    self.send(h, 0, 0, step, axis, 1)
                    self.send(h, 0, 0, 1 - step, axis, -1)

    def arrive(self, h, f, s, sub):
        pltpu.make_async_remote_copy(
            src_ref=self.piece(h, f, s, sub),
            dst_ref=self.piece(h, f, s, sub),
            send_sem=self.ring_send.at[0],
            recv_sem=self.ring_recv.at[self.slot(h, f, s, sub)],
            device_id=self.neighbour(h, 0, 1),
            device_id_type=MESH,
        ).wait_recv()

    def take(self, h, f, s, sub):
        self.arrive(h, f, s, sub)
        if s == 0:
            if f == 3 and sub == 0:
                self.send(h, f, s, sub, 0, 1)
            if f == 1 and sub == 1:
                self.send(h, f, s, sub, 0, -1)
            self.send(h, f, s, sub, 1, 1 if sub == 0 else -1)
            self.send(h, f, s, sub, 1, -1 if sub == 0 else 1)
        else:
            if s == 3 and sub == 0:
                self.send(h, f, s, sub, 1, 1)
            if s == 1 and sub == 1:
                self.send(h, f, s, sub, 1, -1)

    def order(self):
        near = [(3, 0), (1, 1), (3, 1), (1, 0)]
        steps = [(a, 0, sub) for a, sub in near]
        steps += [(0, a, sub) for a, sub in near]
        steps += [(2, 0, 0), (2, 0, 1)]
        for f in (3, 1):
            steps += [(f, a, sub) for a, sub in near]
        steps += [(0, 2, 0), (0, 2, 1)]
        steps += [(2, a, sub) for a, sub in near]
        steps += [(f, 2, sub) for f in (3, 1, 2) for sub in range(2)]
        return [(h, *step) for step in steps for h in range(2)]

    def finish(self):
        for i in range(1, 4):
            self.share(i, False).wait_send()
        for copy in self.sent:
            copy.wait_send()


SPREAD_SEMS = [
    pltpu.SemaphoreType.DMA((4,)),
    pltpu.SemaphoreType.DMA((4,)),
    pltpu.SemaphoreType.DMA((60,)),
    pltpu.SemaphoreType.DMA((64,)),
]


def remote(src, dst, send, recv, to):
    return pltpu.make_async_remote_copy(
        src_ref=src, dst_ref=dst, send_sem=send, recv_sem=recv, device_id=to, device_id_type=MESH
    )


AHEAD = 2
EARLY = 4
FAR_AT = 4


def sigmoid(v):
    return jax.nn.sigmoid(v)


def whole_kernel(
    chain_len, pair_hbm, tri_gain, tri_in, sum_gain, tri_out, att_gain, att_in, att_bias, att_out, new,
    pair, group, edges, left, right, right_all, left_all, left_wide, sums, gates, mid, norm,
    bias_rows, bias, bias_all, norm_all, bias_wide,
    a_s1s, a_s1r, a_rs, a_rr, left_send, left_recv, load,
    b_s1s, b_s1r, b_rs, b_rr, near_sem, far_send, far_recv, fwd_send, fwd_recv,
):
    first = Spread(right, right_all, a_s1s, a_s1r, a_rs, a_rr)
    second = Spread(bias, bias_all, b_s1s, b_s1r, b_rs, b_rr)
    x, zl, y, col = first.x, first.zl, first.y, first.col
    row = lax.axis_index("row")
    sibling = device(x, zl, y, col ^ 1)
    opposite = device(x, zl, y, col ^ 2)
    load_group = pltpu.make_async_copy(pair_hbm.at[:, pl.ds(0, KCD)], group, load.at[0])
    load_pair = pltpu.make_async_copy(pair_hbm, pair, load.at[1])
    load_group.start()
    load_pair.start()
    barrier = pltpu.get_barrier_semaphore()
    count = first.greet(barrier)
    for peer in (sibling, opposite):
        pl.semaphore_signal(barrier, inc=1, device_id=peer, device_id_type=MESH)

    load_group.wait()
    tri_norm = layer_norm(group[...].reshape(256, CH), tri_gain[...]).astype(BF16)
    proj = jnp.dot(tri_norm, tri_in[:, : 4 * CH], preferred_element_type=F32)
    cell = lax.broadcasted_iota(jnp.int32, (256, CH), 0)
    row_live = (row % 4) * 16 + cell // 16 < chain_len[row // 4]
    col_live = cell % 16 < chain_len[col * 4]
    live = jnp.where(row_live, 1.0, 0.0) * jnp.where(col_live, 1.0, 0.0)
    edges[0] = sigmoid(proj[:, :CH]) * proj[:, CH : 2 * CH] * live
    edges[1] = sigmoid(proj[:, 2 * CH : 3 * CH]) * proj[:, 3 * CH :] * live
    for k in range(16):
        left[k] = edges[0, pl.ds(k, 16, stride=16), :].astype(BF16)
        right[k // 8, k % 8] = edges[1, pl.ds(k, 16, stride=16), :].astype(BF16)

    pl.semaphore_wait(barrier, count + 2)
    first.start()
    left_near = remote(left, left_all.at[col], left_send.at[0], left_recv.at[0], sibling)
    left_far = remote(left, left_all.at[col], left_send.at[1], left_recv.at[1], opposite)
    left_near.start()
    left_far.start()
    load_pair.wait()

    def prepare(i, carry):
        normed = layer_norm(pair[i], tri_gain[...]).astype(BF16)
        gates[i] = sigmoid(jnp.dot(normed, tri_in[:, 4 * CH :], preferred_element_type=F32))
        sums[i] = jnp.zeros((16, 16, CH), F32)
        return carry

    lax.fori_loop(0, 6, prepare, 0)
    first.landed(lambda: lax.fori_loop(6, 16, prepare, 0))
    first.own()

    def left_forward(block):
        return remote(
            left_all.at[col ^ 2], left_all.at[block], left_send.at[2], left_recv.at[2], sibling
        )

    remote(left, left_all.at[col ^ 2], left_send.at[1], left_recv.at[1], opposite).wait_recv()
    left_forward(col ^ 2).start()
    remote(left, left_all.at[col ^ 1], left_send.at[0], left_recv.at[0], sibling).wait_recv()
    left_wide[pl.ds(16 * col, 16)] = left[...].astype(F32)
    for j in (1, 2):
        left_wide[pl.ds(16 * (col ^ j), 16)] = left_all[col ^ j].astype(F32)
    left_forward(col ^ 3).wait_recv()
    left_wide[pl.ds(16 * (col ^ 3), 16)] = left_all[col ^ 3].astype(F32)

    def contract(h, f, s):
        xi, yi = (s, f) if h == 0 else (f, s)
        xi, yi = (x + xi) % 4, (y + yi) % 4

        def tile(z, carry):
            part = z * 4 + yi

            def tokens(q, total):
                total = list(total)
                for u in range(2):
                    k = 2 * q + u
                    edge = right_all[h, xi, yi, z, k].astype(F32)
                    for i in range(16):
                        total[i] = total[i] + edge * left_wide[xi * 16 + h * 8 + k, pl.ds(i, 1), :]
                return tuple(total)

            total = lax.fori_loop(0, 4, tokens, tuple(sums[i, part] for i in range(16)))
            for i in range(16):
                sums[i, part] = total[i]
            return carry

        lax.fori_loop(0, 4, tile, 0)

    contract(0, 0, 0)
    contract(1, 0, 0)
    seen = {}
    for h, f, s, sub in first.order():
        first.take(h, f, s, sub)
        seen[(h, f, s)] = seen.get((h, f, s), 0) + 1
        if seen[(h, f, s)] == 2:
            contract(h, f, s)
    first.finish()
    left_near.wait_send()
    left_far.wait_send()
    left_forward(col ^ 2).wait_send()

    def far(r, block):
        return remote(norm.at[r], norm_all.at[block, r], far_send.at[r], far_recv.at[r], opposite)

    def close_row(i):
        sum_norm = layer_norm(sums[i].reshape(256, CH), sum_gain[...]).astype(BF16)
        update = jnp.dot(sum_norm, tri_out[...], preferred_element_type=F32)
        mid_row = (pair[i].astype(F32) + gates[i] * update).astype(BF16)
        mid[i] = mid_row
        att = layer_norm(mid_row, att_gain[...]).astype(BF16)
        norm[i] = att
        norm_all[col, i] = att
        rows = lax.dot_general(att_bias[...], att, (((1,), (1,)), ((), ())), preferred_element_type=F32)
        for h in range(H):
            bias_rows[h, pl.ds(i, 1), :] = rows[h : h + 1]

    def close(i, carry):
        close_row(2 * i)
        close_row(2 * i + 1)

        @pl.when(i < EARLY // 2)
        def _():
            far(2 * i, col).start()
            far(2 * i + 1, col).start()

        return carry

    lax.fori_loop(0, 8, close, 0)
    for h in range(H):
        bias[h // 2, h % 2] = bias_rows[h].astype(BF16)
    second.start()

    def forward(r, block):
        return remote(
            norm_all.at[col ^ 2, r], norm_all.at[block, r], fwd_send.at[r], fwd_recv.at[r], sibling
        )

    def near(block):
        return remote(norm, norm_all.at[block], near_sem.at[0], near_sem.at[1], sibling)

    def pass_on(r):
        far(r, col ^ 2).wait_recv()
        forward(r, col ^ 2).start()

    near(col).start()
    second.landed()
    second.own()

    def far_rest():
        for r in range(EARLY, 16):
            far(r, col).start()

    z_here = (col // 2) * 4 + zl
    edge = (zl == 3) | (z_here == 4)
    pl.when(z_here == 0)(far_rest)
    for at, each in enumerate(second.order()):
        second.take(*each)
        if at == FAR_AT:
            pl.when((z_here != 0) & jnp.logical_not(edge))(far_rest)
        if at == 9:
            pl.when(edge)(far_rest)
    for r in range(AHEAD):
        pass_on(r)
    near(col ^ 1).wait_recv()
    lane = lax.broadcasted_iota(jnp.int32, (16, 256), 1)
    for block in range(4):
        length = jnp.zeros((16, 256), jnp.int32)
        for c in range(4):
            length = jnp.where(lane // SLOT == c, chain_len[block * 4 + c], length)
        masked = jnp.where(lane % SLOT < length, 0.0, NEG_SCORE)
        for h in range(H):
            for part in range(16):
                some = bias_all[h // 2, block, part % 4, part // 4, h % 2].astype(F32)
                bias_wide[h, pl.ds(16 * part, 16), pl.ds(256 * block, 256)] = some + masked
    lane_head = lax.broadcasted_iota(jnp.int32, (256, CH), 1) // DH
    ones = jnp.ones((1024, CH), BF16)

    def attend_row(r):
        here = norm_all[:, r].reshape(4 * 256, CH)
        kv = jnp.dot(here, att_in[:, CH : 3 * CH], preferred_element_type=F32).astype(BF16)
        keys = kv[:, :CH]
        values = jnp.concatenate([kv[:, CH:], ones], axis=1)
        mine = norm[r]
        queries = jnp.dot(mine, att_in[:, :CH], preferred_element_type=F32).astype(BF16)
        gate = jax.nn.sigmoid(jnp.dot(mine, att_in[:, 3 * CH :], preferred_element_type=F32))
        attended = jnp.zeros((256, CH), F32)
        for h in range(H):
            query = jnp.where(lane_head == h, queries, jnp.zeros((), BF16))
            scores = lax.dot_general(
                query, keys, (((1,), (1,)), ((), ())), preferred_element_type=F32
            )
            scores = scores * (1.0 / math.sqrt(DH)) + bias_wide[h]
            top = jnp.max(scores, axis=-1, keepdims=True)
            weights = jnp.exp(scores - top).astype(BF16)
            summed = jnp.dot(weights, values, preferred_element_type=F32)
            attended = jnp.where(lane_head == h, summed[:, :CH] / summed[:, CH:], attended)
        attended = (attended * gate).astype(BF16)
        add = jnp.dot(attended, att_out[...], preferred_element_type=F32)
        new[r] = (mid[r].astype(F32) + add).astype(BF16)

    def attend(q, carry):
        @pl.when(q < 7)
        def _():
            pass_on(2 * q + 2)
            pass_on(2 * q + 3)

        forward(2 * q, col ^ 3).wait_recv()
        forward(2 * q + 1, col ^ 3).wait_recv()
        attend_row(2 * q)
        attend_row(2 * q + 1)
        return carry

    lax.fori_loop(0, 8, attend, 0)
    near(col).wait_send()
    for r in range(16):
        far(r, col).wait_send()
        forward(r, col ^ 2).wait_send()
    second.finish()


ANY = pl.BlockSpec(memory_space=pl.ANY)
VM = pl.BlockSpec(memory_space=pltpu.VMEM)
SM = pl.BlockSpec(memory_space=pltpu.SMEM)


def body(
    pair_rep, chain_len, tri_gain, tri_in, sum_gain, tri_out, att_gain, att_in, att_bias, att_out
):
    vmem = pltpu.VMEM
    return pl.pallas_call(
        whole_kernel,
        name="whole",
        out_shape=jax.ShapeDtypeStruct((16, 256, CH), BF16),
        in_specs=[SM, ANY] + [VM] * 8,
        out_specs=VM,
        scratch_shapes=[
            vmem((16, 256, CH), BF16),
            vmem((16, KCD, CH), BF16),
            vmem((2, 256, CH), F32),
            vmem((16, 16, CH), BF16),
            vmem((2, 8, 16, CH), BF16),
            vmem((2, 4, 4, 4, 8, 16, CH), BF16),
            vmem((4, 16, 16, CH), BF16),
            vmem((64, 16, CH), F32),
            vmem((16, 16, 16, CH), F32),
            vmem((16, 256, CH), F32),
            vmem((16, 256, CH), BF16),
            vmem((16, 256, CH), BF16),
            vmem((H, 16, 256), F32),
            vmem((2, 2, 16, 256), BF16),
            vmem((2, 4, 4, 4, 2, 16, 256), BF16),
            vmem((4, 16, 256, CH), BF16),
            vmem((H, 256, 1024), F32),
        ]
        + SPREAD_SEMS
        + [pltpu.SemaphoreType.DMA((3,)), pltpu.SemaphoreType.DMA((3,)), pltpu.SemaphoreType.DMA((2,))]
        + SPREAD_SEMS
        + [pltpu.SemaphoreType.DMA((2,))]
        + [pltpu.SemaphoreType.DMA((16,))] * 4,
        compiler_params=pltpu.CompilerParams(
            collective_id=0, has_side_effects=True, vmem_limit_bytes=56 << 20
        ),
    )(
        chain_len, pair_rep, tri_gain.reshape(1, CH), tri_in, sum_gain.reshape(1, CH), tri_out,
        att_gain.reshape(1, CH), att_in, att_bias.T, att_out,
    )


def solution(mesh):
    placed = (P("row", "col", None), P(), P(), P(), P(), P(), P(), P(), P(), P())
    return jax.shard_map(
        body, mesh=mesh, in_specs=placed, out_specs=P("row", "col", None), check_vma=False
    )
```

```python
import math

import jax
import jax.numpy as jnp
from jax import lax
from jax.experimental import pallas as pl
from jax.experimental.pallas import tpu as pltpu
from jax.sharding import PartitionSpec as P

CH = 128
H = 4
DH = 32
KCD = 16
SLOT = 64
EPSILON = 1e-05
NEG_SCORE = -1e30
MESH = pl.DeviceIdType.MESH
F32 = jnp.float32
BF16 = jnp.bfloat16


def layer_norm(values, norm_gain):
    values = values.astype(F32)
    centre = values - jnp.mean(values, axis=-1, keepdims=True)
    spread = jnp.mean(centre * centre, axis=-1, keepdims=True)
    return centre * lax.rsqrt(spread + EPSILON) * norm_gain


def place():
    row = lax.axis_index("row")
    col = lax.axis_index("col")
    return row // 16, (row // 4) % 4, row % 4, col


def device(x, zl, y, col):
    return (x * 16 + zl * 4 + y, col)


class Spread:
    def __init__(self, pay, buf, s1_send, s1_recv, ring_send, ring_recv):
        self.pay, self.buf = pay, buf
        self.s1_send, self.s1_recv = s1_send, s1_recv
        self.ring_send, self.ring_recv = ring_send, ring_recv
        self.x, self.zl, self.y, self.col = place()
        self.swapped = self.x != self.col
        self.sent = []

    def partner(self):
        return device(self.col, self.zl, self.y, self.x)

    def line(self, i):
        return device(self.x, (self.zl + i) % 4, self.y, self.col)

    def neighbour(self, h, axis, d):
        along_y = (h == 0) == (axis == 0)
        if along_y:
            return device(self.x, self.zl, (self.y + d + 4) % 4, self.col)
        return device((self.x + d + 4) % 4, self.zl, self.y, self.col)

    def greet(self, barrier):
        def hello(to):
            pl.semaphore_signal(barrier, inc=1, device_id=to, device_id_type=MESH)

        for i in range(1, 4):
            hello(self.line(i))
        for axis in range(2):
            for d in (1, -1):
                hello(self.neighbour(0, axis, d))

        @pl.when(self.swapped)
        def _():
            hello(self.partner())

        return 7 + self.swapped.astype(jnp.int32)

    def swap(self, arrival):
        into = (self.x, self.zl) if arrival else (self.col, self.zl)
        return pltpu.make_async_remote_copy(
            src_ref=self.pay,
            dst_ref=self.buf.at[:, into[0], self.y, into[1]],
            send_sem=self.s1_send.at[0],
            recv_sem=self.s1_recv.at[0],
            device_id=self.partner(),
            device_id_type=MESH,
        )

    def keep(self):
        return pltpu.make_async_copy(
            self.pay, self.buf.at[:, self.x, self.y, self.zl], self.s1_send.at[0]
        )

    def share(self, i, arrival):
        block = self.buf.at[:, self.x, self.y, (self.zl + 4 - i) % 4 if arrival else self.zl]
        return pltpu.make_async_remote_copy(
            src_ref=block,
            dst_ref=block,
            send_sem=self.s1_send.at[i],
            recv_sem=self.s1_recv.at[i],
            device_id=self.line(i),
            device_id_type=MESH,
        )

    def start(self):
        @pl.when(self.swapped)
        def _():
            self.swap(False).start()

        @pl.when(jnp.logical_not(self.swapped))
        def _():
            self.keep().start()

    def landed(self, during=None):
        @pl.when(self.swapped)
        def _():
            self.swap(True).wait_recv()
            self.swap(False).wait_send()

        @pl.when(jnp.logical_not(self.swapped))
        def _():
            self.keep().wait()

        for i in (1, 3, 2):
            self.share(i, False).start()
        if during is not None:
            during()
        for i in (1, 3, 2):
            self.share(i, True).wait_recv()

    def piece(self, h, f, s, sub):
        xi, yi = (s, f) if h == 0 else (f, s)
        return self.buf.at[h, (self.x + xi) % 4, (self.y + yi) % 4, pl.ds(2 * sub, 2)]

    def slot(self, h, f, s, sub):
        return ((h * 4 + f) * 4 + s) * 2 + sub

    def send(self, h, f, s, sub, axis, d):
        there = ((f - d) % 4, s) if axis == 0 else (f, (s - d) % 4)
        copy = pltpu.make_async_remote_copy(
            src_ref=self.piece(h, f, s, sub),
            dst_ref=self.piece(h, f, s, sub),
            send_sem=self.ring_send.at[len(self.sent)],
            recv_sem=self.ring_recv.at[self.slot(h, *there, sub)],
            device_id=self.neighbour(h, axis, d),
            device_id_type=MESH,
        )
        copy.start()
        self.sent.append(copy)

    def own(self):
        for axis in range(2):
            for step in range(2):
                for h in range(2):
                    self.send(h, 0, 0, step, axis, 1)
                    self.send(h, 0, 0, 1 - step, axis, -1)

    def arrive(self, h, f, s, sub):
        pltpu.make_async_remote_copy(
            src_ref=self.piece(h, f, s, sub),
            dst_ref=self.piece(h, f, s, sub),
            send_sem=self.ring_send.at[0],
            recv_sem=self.ring_recv.at[self.slot(h, f, s, sub)],
            device_id=self.neighbour(h, 0, 1),
            device_id_type=MESH,
        ).wait_recv()

    def take(self, h, f, s, sub):
        self.arrive(h, f, s, sub)
        if s == 0:
            if f == 3 and sub == 0:
                self.send(h, f, s, sub, 0, 1)
            if f == 1 and sub == 1:
                self.send(h, f, s, sub, 0, -1)
            self.send(h, f, s, sub, 1, 1 if sub == 0 else -1)
            self.send(h, f, s, sub, 1, -1 if sub == 0 else 1)
        else:
            if s == 3 and sub == 0:
                self.send(h, f, s, sub, 1, 1)
            if s == 1 and sub == 1:
                self.send(h, f, s, sub, 1, -1)

    def order(self):
        near = [(3, 0), (1, 1), (3, 1), (1, 0)]
        steps = [(a, 0, sub) for a, sub in near]
        steps += [(0, a, sub) for a, sub in near]
        steps += [(2, 0, 0), (2, 0, 1)]
        for f in (3, 1):
            steps += [(f, a, sub) for a, sub in near]
        steps += [(0, 2, 0), (0, 2, 1)]
        steps += [(2, a, sub) for a, sub in near]
        steps += [(f, 2, sub) for f in (3, 1, 2) for sub in range(2)]
        return [(h, *step) for step in steps for h in range(2)]

    def finish(self):
        for i in range(1, 4):
            self.share(i, False).wait_send()
        for copy in self.sent:
            copy.wait_send()


SPREAD_SEMS = [
    pltpu.SemaphoreType.DMA((4,)),
    pltpu.SemaphoreType.DMA((4,)),
    pltpu.SemaphoreType.DMA((60,)),
    pltpu.SemaphoreType.DMA((64,)),
]


def remote(src, dst, send, recv, to):
    return pltpu.make_async_remote_copy(
        src_ref=src, dst_ref=dst, send_sem=send, recv_sem=recv, device_id=to, device_id_type=MESH
    )


AHEAD = 2
EARLY = 4
FAR_AT = 4


def sigmoid(v):
    return jax.nn.sigmoid(v)


def whole_kernel(
    chain_len, pair_hbm, tri_gain, tri_in, sum_gain, tri_out, att_gain, att_in, att_bias, att_out, new,
    pair, group, edges, left, right, right_all, left_all, left_wide, sums, gates, mid, norm,
    bias_rows, bias, bias_all, norm_all, bias_wide,
    a_s1s, a_s1r, a_rs, a_rr, left_send, left_recv, load,
    b_s1s, b_s1r, b_rs, b_rr, near_sem, far_send, far_recv, fwd_send, fwd_recv,
):
    first = Spread(right, right_all, a_s1s, a_s1r, a_rs, a_rr)
    second = Spread(bias, bias_all, b_s1s, b_s1r, b_rs, b_rr)
    x, zl, y, col = first.x, first.zl, first.y, first.col
    row = lax.axis_index("row")
    sibling = device(x, zl, y, col ^ 1)
    opposite = device(x, zl, y, col ^ 2)
    load_group = pltpu.make_async_copy(pair_hbm.at[:, pl.ds(0, KCD)], group, load.at[0])
    load_pair = pltpu.make_async_copy(pair_hbm, pair, load.at[1])
    load_group.start()
    load_pair.start()
    barrier = pltpu.get_barrier_semaphore()
    count = first.greet(barrier)
    for peer in (sibling, opposite):
        pl.semaphore_signal(barrier, inc=1, device_id=peer, device_id_type=MESH)

    load_group.wait()
    tri_norm = layer_norm(group[...].reshape(256, CH), tri_gain[...]).astype(BF16)
    proj = jnp.dot(tri_norm, tri_in[:, : 4 * CH], preferred_element_type=F32)
    cell = lax.broadcasted_iota(jnp.int32, (256, CH), 0)
    row_live = (row % 4) * 16 + cell // 16 < chain_len[row // 4]
    col_live = cell % 16 < chain_len[col * 4]
    live = jnp.where(row_live, 1.0, 0.0) * jnp.where(col_live, 1.0, 0.0)
    edges[0] = sigmoid(proj[:, :CH]) * proj[:, CH : 2 * CH] * live
    edges[1] = sigmoid(proj[:, 2 * CH : 3 * CH]) * proj[:, 3 * CH :] * live
    for k in range(16):
        left[k] = edges[0, pl.ds(k, 16, stride=16), :].astype(BF16)
        right[k // 8, k % 8] = edges[1, pl.ds(k, 16, stride=16), :].astype(BF16)

    pl.semaphore_wait(barrier, count + 2)
    first.start()
    left_near = remote(left, left_all.at[col], left_send.at[0], left_recv.at[0], sibling)
    left_far = remote(left, left_all.at[col], left_send.at[1], left_recv.at[1], opposite)
    left_near.start()
    left_far.start()
    load_pair.wait()

    def prepare(i, carry):
        normed = layer_norm(pair[i], tri_gain[...]).astype(BF16)
        gates[i] = sigmoid(jnp.dot(normed, tri_in[:, 4 * CH :], preferred_element_type=F32))
        sums[i] = jnp.zeros((16, 16, CH), F32)
        return carry

    lax.fori_loop(0, 6, prepare, 0)
    first.landed(lambda: lax.fori_loop(6, 16, prepare, 0))
    first.own()

    def left_forward(block):
        return remote(
            left_all.at[col ^ 2], left_all.at[block], left_send.at[2], left_recv.at[2], sibling
        )

    remote(left, left_all.at[col ^ 2], left_send.at[1], left_recv.at[1], opposite).wait_recv()
    left_forward(col ^ 2).start()
    remote(left, left_all.at[col ^ 1], left_send.at[0], left_recv.at[0], sibling).wait_recv()
    left_wide[pl.ds(16 * col, 16)] = left[...].astype(F32)
    for j in (1, 2):
        left_wide[pl.ds(16 * (col ^ j), 16)] = left_all[col ^ j].astype(F32)
    left_forward(col ^ 3).wait_recv()
    left_wide[pl.ds(16 * (col ^ 3), 16)] = left_all[col ^ 3].astype(F32)

    def contract(h, f, s):
        xi, yi = (s, f) if h == 0 else (f, s)
        xi, yi = (x + xi) % 4, (y + yi) % 4

        def tile(z, carry):
            part = z * 4 + yi

            def tokens(q, total):
                total = list(total)
                for u in range(2):
                    k = 2 * q + u
                    edge = right_all[h, xi, yi, z, k].astype(F32)
                    for i in range(16):
                        total[i] = total[i] + edge * left_wide[xi * 16 + h * 8 + k, pl.ds(i, 1), :]
                return tuple(total)

            total = lax.fori_loop(0, 4, tokens, tuple(sums[i, part] for i in range(16)))
            for i in range(16):
                sums[i, part] = total[i]
            return carry

        lax.fori_loop(0, 4, tile, 0)

    contract(0, 0, 0)
    contract(1, 0, 0)
    seen = {}
    for h, f, s, sub in first.order():
        first.take(h, f, s, sub)
        seen[(h, f, s)] = seen.get((h, f, s), 0) + 1
        if seen[(h, f, s)] == 2:
            contract(h, f, s)

    def far(r, block):
        return remote(norm.at[r], norm_all.at[block, r], far_send.at[r], far_recv.at[r], opposite)

    def close_row(i):
        sum_norm = layer_norm(sums[i].reshape(256, CH), sum_gain[...]).astype(BF16)
        update = jnp.dot(sum_norm, tri_out[...], preferred_element_type=F32)
        mid_row = (pair[i].astype(F32) + gates[i] * update).astype(BF16)
        mid[i] = mid_row
        att = layer_norm(mid_row, att_gain[...]).astype(BF16)
        norm[i] = att
        norm_all[col, i] = att
        rows = lax.dot_general(att_bias[...], att, (((1,), (1,)), ((), ())), preferred_element_type=F32)
        for h in range(H):
            bias_rows[h, pl.ds(i, 1), :] = rows[h : h + 1]

    def close(i, carry):
        close_row(2 * i)
        close_row(2 * i + 1)

        @pl.when(i < EARLY // 2)
        def _():
            far(2 * i, col).start()
            far(2 * i + 1, col).start()

        return carry

    lax.fori_loop(0, 8, close, 0)
    for h in range(H):
        bias[h // 2, h % 2] = bias_rows[h].astype(BF16)
    second.start()

    def forward(r, block):
        return remote(
            norm_all.at[col ^ 2, r], norm_all.at[block, r], fwd_send.at[r], fwd_recv.at[r], sibling
        )

    def near(block):
        return remote(norm, norm_all.at[block], near_sem.at[0], near_sem.at[1], sibling)

    def pass_on(r):
        far(r, col ^ 2).wait_recv()
        forward(r, col ^ 2).start()

    near(col).start()
    second.landed()
    second.own()

    def far_rest():
        for r in range(EARLY, 16):
            far(r, col).start()

    z_here = (col // 2) * 4 + zl
    edge = (zl == 3) | (z_here == 4)
    pl.when(z_here == 0)(far_rest)
    for at, each in enumerate(second.order()):
        second.take(*each)
        if at == FAR_AT:
            pl.when((z_here != 0) & jnp.logical_not(edge))(far_rest)
        if at == 9:
            pl.when(edge)(far_rest)
    for r in range(AHEAD):
        pass_on(r)
    near(col ^ 1).wait_recv()
    lane = lax.broadcasted_iota(jnp.int32, (16, 256), 1)
    for block in range(4):
        length = jnp.zeros((16, 256), jnp.int32)
        for c in range(4):
            length = jnp.where(lane // SLOT == c, chain_len[block * 4 + c], length)
        masked = jnp.where(lane % SLOT < length, 0.0, NEG_SCORE)
        for h in range(H):
            for part in range(16):
                some = bias_all[h // 2, block, part % 4, part // 4, h % 2].astype(F32)
                bias_wide[h, pl.ds(16 * part, 16), pl.ds(256 * block, 256)] = some + masked
    lane_head = lax.broadcasted_iota(jnp.int32, (256, CH), 1) // DH
    ones = jnp.ones((1024, CH), BF16)

    def attend_row(r):
        here = norm_all[:, r].reshape(4 * 256, CH)
        kv = jnp.dot(here, att_in[:, CH : 3 * CH], preferred_element_type=F32).astype(BF16)
        keys = kv[:, :CH]
        values = jnp.concatenate([kv[:, CH:], ones], axis=1)
        mine = norm[r]
        queries = jnp.dot(mine, att_in[:, :CH], preferred_element_type=F32).astype(BF16)
        gate = jax.nn.sigmoid(jnp.dot(mine, att_in[:, 3 * CH :], preferred_element_type=F32))
        attended = jnp.zeros((256, CH), F32)
        for h in range(H):
            query = jnp.where(lane_head == h, queries, jnp.zeros((), BF16))
            scores = lax.dot_general(
                query, keys, (((1,), (1,)), ((), ())), preferred_element_type=F32
            )
            scores = scores * (1.0 / math.sqrt(DH)) + bias_wide[h]
            top = jnp.max(scores, axis=-1, keepdims=True)
            weights = jnp.exp(scores - top).astype(BF16)
            summed = jnp.dot(weights, values, preferred_element_type=F32)
            attended = jnp.where(lane_head == h, summed[:, :CH] / summed[:, CH:], attended)
        attended = (attended * gate).astype(BF16)
        add = jnp.dot(attended, att_out[...], preferred_element_type=F32)
        new[r] = (mid[r].astype(F32) + add).astype(BF16)

    def attend(q, carry):
        @pl.when(q < 7)
        def _():
            pass_on(2 * q + 2)
            pass_on(2 * q + 3)

        forward(2 * q, col ^ 3).wait_recv()
        forward(2 * q + 1, col ^ 3).wait_recv()
        attend_row(2 * q)
        attend_row(2 * q + 1)
        return carry

    lax.fori_loop(0, 8, attend, 0)
    near(col).wait_send()
    for r in range(16):
        far(r, col).wait_send()
        forward(r, col ^ 2).wait_send()
    second.finish()
    first.finish()
    left_near.wait_send()
    left_far.wait_send()
    left_forward(col ^ 2).wait_send()


ANY = pl.BlockSpec(memory_space=pl.ANY)
VM = pl.BlockSpec(memory_space=pltpu.VMEM)
SM = pl.BlockSpec(memory_space=pltpu.SMEM)


def body(
    pair_rep, chain_len, tri_gain, tri_in, sum_gain, tri_out, att_gain, att_in, att_bias, att_out
):
    vmem = pltpu.VMEM
    return pl.pallas_call(
        whole_kernel,
        name="whole",
        out_shape=jax.ShapeDtypeStruct((16, 256, CH), BF16),
        in_specs=[SM, ANY] + [VM] * 8,
        out_specs=VM,
        scratch_shapes=[
            vmem((16, 256, CH), BF16),
            vmem((16, KCD, CH), BF16),
            vmem((2, 256, CH), F32),
            vmem((16, 16, CH), BF16),
            vmem((2, 8, 16, CH), BF16),
            vmem((2, 4, 4, 4, 8, 16, CH), BF16),
            vmem((4, 16, 16, CH), BF16),
            vmem((64, 16, CH), F32),
            vmem((16, 16, 16, CH), F32),
            vmem((16, 256, CH), F32),
            vmem((16, 256, CH), BF16),
            vmem((16, 256, CH), BF16),
            vmem((H, 16, 256), F32),
            vmem((2, 2, 16, 256), BF16),
            vmem((2, 4, 4, 4, 2, 16, 256), BF16),
            vmem((4, 16, 256, CH), BF16),
            vmem((H, 256, 1024), F32),
        ]
        + SPREAD_SEMS
        + [pltpu.SemaphoreType.DMA((3,)), pltpu.SemaphoreType.DMA((3,)), pltpu.SemaphoreType.DMA((2,))]
        + SPREAD_SEMS
        + [pltpu.SemaphoreType.DMA((2,))]
        + [pltpu.SemaphoreType.DMA((16,))] * 4,
        compiler_params=pltpu.CompilerParams(
            collective_id=0, has_side_effects=True, vmem_limit_bytes=56 << 20
        ),
    )(
        chain_len, pair_rep, tri_gain.reshape(1, CH), tri_in, sum_gain.reshape(1, CH), tri_out,
        att_gain.reshape(1, CH), att_in, att_bias.T, att_out,
    )


def solution(mesh):
    placed = (P("row", "col", None), P(), P(), P(), P(), P(), P(), P(), P(), P())
    return jax.shard_map(
        body, mesh=mesh, in_specs=placed, out_specs=P("row", "col", None), check_vma=False
    )
```
